32 devices in a mesh: space: 4 (over y, core), dir: 8 (over z, x).
Axes of the slice: x: 2, y: 2, z: 4, core: 2. Of those that a mesh axis runs over, the one named last changes fastest.
Arguments:
- multipoles: bfloat16 [2048, 256], P(('space', 'dir')), may hold values from -6 to 6
- box_scale: float32 [2048], P(('space', 'dir')), may hold values from 0.5 to 2
- fine_list: int32 [2048, 32], P(('space', 'dir')), may hold values from 0 to 2047, as said below
- wedge_index: int32 [2048, 32], P(('space', 'dir')), may hold values from 0 to 15
- list_count: int32 [2048], P(('space', 'dir')), may hold values from 16 to 32
- fine_ops: bfloat16 [16, 256, 256], replicated, may hold values from -0.1875 to 0.1875
- phases: float32 [16, 128], replicated, may hold values from -3.140625 to 3.140625
- coarse_list: int32 [16, 2048, 4], P('dir', 'space'), may hold values from 0 to 511
- coarse_ops: bfloat16 [16, 256, 256], P('dir'), may hold values from -0.1875 to 0.1875
Outputs:
- fine_local: float32 [2048, 256], P(('space', 'dir'))
- coarse_local: bfloat16 [16, 2048, 256], P(None, ('space', 'dir'))
The draws below stay inside these ranges and needn't reach their ends.
Inputs may be any that keep to these rules, and one draw needn't show every extreme that they name: `fine_list`: each entry is the global id of a box of the same subtree as the list's box, or a box of the neighbouring subtree (one index of space up or down) held by the same index of dir; box ids run over space, then dir, then 64 boxes of a device.
All inputs are finite; a program needn't handle non-finite values.
Results may differ from the reference program's by a relative error of at most 0.018.
Values may be sent and summed in bfloat16 or wider, within the bound.
A program may use at most 64 MiB of HBM per device.

```python
import math
import jax
import jax.numpy as jnp
from jax import lax

COEFFS = 256
WEDGES = 16
FLIST = 32
CLIST = 4
BOX_DEV = 64
DIRS = 16
GROUP_BOXES = 512
BOXES = 2048
N_SPACE = 4
N_DIR = 8


def draw_fine_list(key, part):
    first_key, second_key, third_key = jax.random.split(jax.random.fold_in(key, 11), 3)
    box_ids = jnp.arange(BOXES, dtype=jnp.int32)[:, None]
    subtree = box_ids // GROUP_BOXES
    dir_slot = box_ids // BOX_DEV % (GROUP_BOXES // BOX_DEV)
    kinds = jax.random.randint(first_key, (BOXES, FLIST), 0, 4)
    same_tree = jax.random.randint(second_key, (BOXES, FLIST), 0, GROUP_BOXES) + subtree * GROUP_BOXES
    near_slot = jax.random.randint(third_key, (BOXES, FLIST), 0, BOX_DEV)
    below = (subtree - 1) * GROUP_BOXES + dir_slot * BOX_DEV + near_slot
    above = (subtree + 1) * GROUP_BOXES + dir_slot * BOX_DEV + near_slot
    use_below = (kinds == 2) & (subtree > 0)
    use_above = (kinds == 3) & (subtree < N_SPACE - 1)
    return jnp.where(use_below, below, jnp.where(use_above, above, same_tree)).astype(jnp.int32)


def set_ends(array, stream_key, low, largest):
    longest = array.shape.index(max(array.shape))
    spots = []
    for shift in (0, 1):
        where = [jax.random.randint(jax.random.fold_in(stream_key, axis), (), 0, length) for axis, length in enumerate(array.shape)]
        where[longest] = (where[longest] + shift) % array.shape[longest]
        spots.append(tuple(where))
    return array.at[spots[0]].set(low).at[spots[1]].set(largest)


def block_scale(stream_key, extent, cuts, low, high):
    def one(axis_at, blocks):
        heights = jax.random.uniform(jax.random.fold_in(jax.random.fold_in(stream_key, 6), axis_at), (blocks,), jnp.float32, low / len(cuts), high / len(cuts))
        return jnp.repeat(jnp.exp(heights), extent[axis_at] // blocks).reshape((-1,) + (1,) * (len(extent) - axis_at - 1))

    loudness = one(*cuts[0])
    for cut in cuts[1:]:
        loudness = loudness * one(*cut)
    return loudness


def bell_draw(own_key, dims, scale, limit, pieces=(), kind=jnp.bfloat16):
    drawn = scale * jax.random.normal(own_key, dims, jnp.float32)
    if pieces:
        drawn = drawn * block_scale(own_key, dims, pieces, -0.22, 0.18)
    return jnp.clip(drawn, -limit, limit).astype(kind)


def setup_inputs(seed: int = 0) -> dict:
    key_list = jax.random.split(jax.random.key(seed), 10)
    multipoles = bell_draw(key_list[0], (BOXES, COEFFS), 1.0, 6.0, ((0, 32),))
    box_scale = jnp.clip(jnp.exp(math.log(2.0) - 1.3862944 * jax.random.uniform(key_list[1], (BOXES,), jnp.float32) ** block_scale(key_list[1], (BOXES,), ((0, 32),), -0.2, 0.2)), 0.5, 2.0)
    fine_list = draw_fine_list(jax.random.fold_in(key_list[9], 71), 0)
    wedge_index = set_ends(jax.random.randint(key_list[3], (BOXES, FLIST), 0, WEDGES), jax.random.fold_in(key_list[3], 1), 0, WEDGES - 1).astype(jnp.int32)
    list_count = set_ends(jax.random.randint(key_list[4], (BOXES,), FLIST // 2, FLIST + 1), jax.random.fold_in(key_list[4], 1), FLIST // 2, FLIST).astype(jnp.int32)
    fine_ops = bell_draw(key_list[5], (WEDGES, COEFFS, COEFFS), (COEFFS * 4) ** -0.5, 0.1875)
    phases = jnp.clip(jax.random.uniform(key_list[6], (DIRS, COEFFS // 2), jnp.float32, -3.140625, 3.140625), -3.140625, 3.140625)
    coarse_list = set_ends(jax.random.randint(key_list[7], (DIRS, BOXES, CLIST), 0, GROUP_BOXES), jax.random.fold_in(key_list[7], 1), 0, GROUP_BOXES - 1).astype(jnp.int32)
    coarse_ops = bell_draw(key_list[8], (DIRS, COEFFS, COEFFS), (COEFFS * CLIST) ** -0.5, 0.1875, ((0, 8),))
    return dict(multipoles=multipoles, box_scale=box_scale, fine_list=fine_list, wedge_index=wedge_index, list_count=list_count, fine_ops=fine_ops, phases=phases, coarse_list=coarse_list, coarse_ops=coarse_ops)


def directional(picked, angles):
    half_width = picked.shape[-1] // 2
    real_part = picked[..., :half_width].astype(jnp.float32)
    imag_part = picked[..., half_width:].astype(jnp.float32)
    cosine = jnp.cos(angles)
    sine = jnp.sin(angles)
    return jnp.concatenate([real_part * cosine - imag_part * sine, real_part * sine + imag_part * cosine], axis=-1).astype(jnp.bfloat16)


def reference(multipoles, box_scale, fine_list, wedge_index, list_count, fine_ops, phases, coarse_list, coarse_ops):
    blocks = N_SPACE * N_DIR
    wedge_ids = jnp.arange(WEDGES, dtype=jnp.int32)
    slot_ids = jnp.arange(FLIST, dtype=jnp.int32)
    fine_matrices = fine_ops.astype(jnp.float32)

    def fine_block(inputs):
        source_ids, wedges, counts = inputs
        picked = multipoles[source_ids].astype(jnp.float32)
        in_count = slot_ids[None, :] < counts[:, None]
        wedge_mask = ((wedges[:, :, None] == wedge_ids[None, None, :]) & in_count[:, :, None]).astype(jnp.float32)
        wedge_sums = jnp.einsum('bjw,bjp->bwp', wedge_mask, picked, precision=lax.Precision.HIGHEST).astype(jnp.bfloat16)
        return jnp.einsum('bwp,wpq->bq', wedge_sums.astype(jnp.float32), fine_matrices, precision=lax.Precision.HIGHEST)

    fine_local = lax.map(fine_block, (fine_list.reshape(blocks, BOX_DEV, FLIST), wedge_index.reshape(blocks, BOX_DEV, FLIST), list_count.reshape(blocks, BOX_DEV)))
    fine_local = fine_local.reshape(BOXES, COEFFS)

    group_start = (jnp.arange(BOXES, dtype=jnp.int32) // GROUP_BOXES) * GROUP_BOXES

    def coarse_direction(inputs):
        box_lists, matrix, angles = inputs
        accumulated = jnp.zeros((BOXES, COEFFS), jnp.float32)
        for term_index in range(CLIST):
            source_ids = (box_lists[:, term_index] + group_start).astype(jnp.int32)
            source_angles = angles[None, :] * box_scale[source_ids][:, None]
            accumulated = accumulated + directional(multipoles[source_ids], source_angles).astype(jnp.float32)
        gathered = accumulated.astype(jnp.bfloat16)
        return jnp.dot(gathered, matrix, preferred_element_type=jnp.float32).astype(jnp.bfloat16)

    coarse_local = lax.map(coarse_direction, (coarse_list, coarse_ops, phases))
    return fine_local, coarse_local
```

```python
import functools
import math

import jax
import jax.numpy as jnp
from jax import lax
from jax.experimental import pallas as pl
from jax.experimental.pallas import tpu as pltpu
from jax.sharding import PartitionSpec as P

MESH = pl.DeviceIdType.MESH
F32 = jnp.float32
BF16 = jnp.bfloat16
LANES = 128
HALF_TURN_HI = 3.140625
HALF_TURN_LO = 9.67653589793e-4
SINE = (1.0, -0.1666666716337204, 0.008333330973982811, -0.00019840856839437038,
        2.752503405645257e-06, -2.388494557692411e-08)
COSINE = (1.0, -0.5, 0.0416666679084301, -0.0013888884568586946, 2.4801034669508226e-05,
          -2.7524427537174332e-07, 1.9903911852026113e-09)


def horner(terms, x):
    total = jnp.full_like(x, terms[-1])
    for term in terms[-2::-1]:
        total = total * x + term
    return total


def signed_turn(angle):
    turns = jnp.floor(angle * (1.0 / math.pi) + 0.5)
    rest = (angle - turns * HALF_TURN_HI) - turns * HALF_TURN_LO
    halves = turns * 0.5
    sign = 1.0 - 4.0 * (halves - jnp.floor(halves))
    square = rest * rest
    return sign, horner(COSINE, square), horner(SINE, square) * rest


def partner(me, k):
    bit, other = 1, me
    while bit <= k:
        if k & bit:
            other = other + bit * (1 - 2 * ((me // bit) % 2))
        bit *= 2
    return other


def kernel(n_dir, n_space, boxes, dirs, block_boxes, mult, scale, lists, fine_list, wedge_index, list_count, phases,
           fine_ops, coarse_ops,
           fine_out, coarse_out,
           cand, scales, lists_v, far_lists, fine_v, wedge_v, count_v, slots_v, phases_v, fine_ops_v, coarse_ops_v, far_ops,
           columns, counts, weights, rotated, sums, translated,
           local_sem, rows_send, rows_recv, scale_send, scale_recv, halo_send, halo_recv, list_sems, ops_send, ops_recv,
           back_send, back_recv):
    me = lax.axis_index("dir")
    space = lax.axis_index("space")
    group = n_dir * boxes
    half = n_dir // 2
    inside = half * boxes
    width = mult.shape[1] // 2
    terms = lists.shape[1]
    wedges = fine_ops.shape[0]
    own = pl.ds(pl.multiple_of(me * boxes, boxes), boxes)
    above = lax.rem(space + 1, n_space)
    below = lax.rem(space + n_space - 1, n_space)
    core = lax.rem(space, 2)
    sibling = space + 1 - 2 * core
    far = partner(me, half)
    base = me // half * half
    first_inside = pl.multiple_of(base * boxes, inside)
    first_far = pl.multiple_of((half - base) * boxes, inside)
    share_dirs = dirs // 2
    share = pl.ds(core * share_dirs, share_dirs)

    barrier = pltpu.get_barrier_semaphore()
    for k in range(1, half + 1):
        pl.semaphore_signal(barrier, inc=1, device_id={"dir": partner(me, k)}, device_id_type=MESH)
    for other in (above, below):
        pl.semaphore_signal(barrier, inc=1, device_id={"space": other}, device_id_type=MESH)

    pulls = [
        pltpu.make_async_copy(lists.at[:, :, pl.ds(first_inside, inside)], lists_v, local_sem.at[0]),
        pltpu.make_async_copy(fine_list, fine_v, local_sem.at[1]),
        pltpu.make_async_copy(wedge_index, wedge_v, local_sem.at[2]),
        pltpu.make_async_copy(mult, cand.at[own], local_sem.at[3]),
        pltpu.make_async_copy(scale, scales.at[me], local_sem.at[4]),
        pltpu.make_async_copy(phases, phases_v, local_sem.at[5]),
        pltpu.make_async_copy(coarse_ops, coarse_ops_v, local_sem.at[6]),
        pltpu.make_async_copy(fine_ops, fine_ops_v, local_sem.at[7]),
        pltpu.make_async_copy(list_count, count_v, local_sem.at[8]),
    ]
    for at in (3, 4, 0, 6, 1, 2, 8, 5, 7):
        pulls[at].start()

    def set_columns(values):
        columns[...] = jnp.transpose(
            jnp.concatenate([values[d].astype(F32) for d in range(dirs)], axis=0))

    def set_counts(first_slot):
        def count_rows(i, carry):
            rows = pl.ds(pl.multiple_of(i * boxes, boxes), boxes)
            ids = columns[rows, :]
            lane = lax.broadcasted_iota(jnp.int32, (boxes, group), 1).astype(F32)
            for d in range(dirs):
                total = jnp.zeros((boxes, group), F32)
                for k in range(terms):
                    at = d * terms + k
                    total = total + jnp.where(ids[:, at:at + 1] == lane, 1.0, 0.0)
                counts[first_slot + d, rows, :] = total.astype(BF16)
            return carry

        lax.fori_loop(0, half, count_rows, 0)

    pulls[0].wait()
    set_columns(lists_v)
    pulls[3].wait()
    pulls[4].wait()

    pl.semaphore_wait(barrier, half + 2)

    row_copies, scale_copies = {}, {}

    def send_block(k, to, source):
        rows = pl.ds(pl.multiple_of(source * boxes, boxes), boxes)
        row_copies[k] = pltpu.make_async_remote_copy(
            cand.at[rows], cand.at[rows], rows_send.at[k], rows_recv.at[k],
            device_id={"dir": partner(me, to)}, device_id_type=MESH)
        row_copies[k].start()
        scale_copies[k] = pltpu.make_async_remote_copy(
            scales.at[source], scales.at[source], scale_send.at[k], scale_recv.at[k],
            device_id={"dir": partner(me, to)}, device_id_type=MESH)
        scale_copies[k].start()

    send_block(half, half, me)
    for k in range(half - 1, 0, -1):
        send_block(k, k, me)
    list_copy = pltpu.make_async_remote_copy(
        lists.at[:, :, pl.ds(first_far, inside)], far_lists, list_sems.at[0], list_sems.at[1],
        device_id={"dir": far}, device_id_type=MESH)
    list_copy.start()
    halos = []
    for side, other in ((0, above), (1, below)):
        halos.append(pltpu.make_async_remote_copy(
            cand.at[own], cand.at[pl.ds(group + side * boxes, boxes)], halo_send.at[side], halo_recv.at[side],
            device_id={"space": other}, device_id_type=MESH))
        halos[-1].start()
    pulls[6].wait()
    ops_copies = [pltpu.make_async_remote_copy(
        coarse_ops_v.at[share], far_ops.at[share], ops_send.at[0], ops_recv.at[0],
        device_id={"dir": far}, device_id_type=MESH)]
    ops_copies[0].start()

    set_counts(0)

    pulls[1].wait()
    pulls[2].wait()
    pulls[8].wait()
    blocks = boxes // block_boxes
    members = block_boxes * wedges
    width_list = fine_v.shape[0]
    first = fine_v[...] - space * group
    slot_values = jnp.where(
        first < 0, first + (2 * group - me * boxes), jnp.where(first < group, first, first + (boxes - me * boxes)))
    box = lax.broadcasted_iota(jnp.int32, (width_list, boxes), 1)
    term = lax.broadcasted_iota(jnp.int32, (width_list, boxes), 0)
    code_values = jnp.where(term < count_v[...], wedge_v[...] * block_boxes + box % block_boxes, -1)
    packs = LANES // block_boxes
    depth = width_list // packs
    blank = jnp.zeros((width_list, LANES - boxes), jnp.int32)
    slots_v[0] = jnp.concatenate([slot_values, blank], axis=1)
    slots_v[1] = jnp.concatenate([code_values, blank], axis=1)
    pack = lax.broadcasted_iota(jnp.int32, (depth, LANES), 1) // block_boxes

    def cells_of(which, g):
        row = jnp.zeros((depth, LANES), jnp.int32)
        for p in range(packs):
            row = jnp.where(pack == (g + p) % packs, turned[which][p], row)
        if g:
            row = pltpu.roll(row, LANES - g * block_boxes, 1)
        return jnp.concatenate([row[t:t + 1, :] for t in range(depth)], axis=1)

    turned = []
    for which in range(2):
        pieces = [slots_v[which, p * depth:(p + 1) * depth, :] for p in range(packs)]
        turned.append([pieces[0]] + [pltpu.roll(pieces[p], p * block_boxes, 1) for p in range(1, packs)])
    cells = depth * LANES
    for g in range(blocks):
        member = lax.broadcasted_iota(jnp.int32, (members, cells), 0)
        mask = jnp.where(member == cells_of(1, g), 1.0, 0.0).astype(BF16)
        candidate = lax.broadcasted_iota(jnp.int32, (cand.shape[0], cells), 0)
        onehot = jnp.where(candidate == cells_of(0, g), 1.0, 0.0).astype(BF16)
        weights[g * members:(g + 1) * members, :] = lax.dot_general(
            mask, onehot, (((1,), (1,)), ((), ())), preferred_element_type=F32).astype(BF16)

    pulls[5].wait()

    def rotate(source):
        rows = pl.ds(pl.multiple_of(source * boxes, boxes), boxes)
        column = jnp.transpose(jnp.broadcast_to(scales[source], (8, boxes)))[:, 0:1]
        picked = cand[rows, :].astype(F32)
        real, imag = picked[:, :width], picked[:, width:]
        for slot in range(2 * dirs):
            owner = me if slot < dirs else far
            angle = phases_v[pl.ds(owner * dirs + slot % dirs, 1), :] * column
            sign, cosine, sine = signed_turn(angle)
            cosine, sine = cosine * sign, sine * sign
            rotated[slot, rows, :width] = (real * cosine - imag * sine).astype(BF16)
            rotated[slot, rows, width:] = (real * sine + imag * cosine).astype(BF16)

    def arrived(k):
        row_copies[k].wait_recv()
        scale_copies[k].wait_recv()

    rotate(me)
    arrived(1)
    rotate(partner(me, 1))
    arrived(half)
    for k in range(half - 1, 0, -1):
        send_block(half + k, k, far)
    for k in range(2, half):
        arrived(k)
        rotate(partner(me, k))
    rotate(far)
    list_copy.wait_recv()
    set_columns(far_lists)
    set_counts(dirs)
    for k in range(half + 1, n_dir):
        arrived(k)
        rotate(partner(me, k))

    backs, keeps = [], []

    def translate(slot, d, at, matrix, owner):
        gathered = jnp.dot(counts[at], rotated[at], preferred_element_type=F32).astype(BF16)
        result = jnp.dot(gathered, matrix, preferred_element_type=F32).astype(BF16)
        for member in range(half):
            translated[slot, member] = result[member * boxes:(member + 1) * boxes]
        here = coarse_out.at[owner * dirs + d]
        for k in range(half - 1, 0, -1):
            to = partner(me, k)
            backs.append(pltpu.make_async_remote_copy(
                translated.at[slot, to - base], here, back_send.at[slot, k], back_recv.at[slot, k],
                device_id={"dir": to}, device_id_type=MESH))
            backs[-1].start()
        keeps.append(pltpu.make_async_copy(translated.at[slot, me - base], here, back_recv.at[slot, 0]))
        keeps[-1].start()

    for d in range(dirs):
        translate(d, d, d, coarse_ops_v[d], me)
    ops_copies[0].wait_recv()
    ops_copies.append(pltpu.make_async_remote_copy(
        far_ops.at[share], far_ops.at[share], ops_send.at[1], ops_recv.at[1],
        device_id={"space": sibling}, device_id_type=MESH))
    ops_copies[1].start()
    for i in range(share_dirs):
        d = core * share_dirs + i
        translate(dirs + i, d, dirs + d, far_ops[d], far)
    ops_copies[1].wait_recv()
    for i in range(share_dirs):
        d = (1 - core) * share_dirs + i
        translate(dirs + share_dirs + i, d, dirs + d, far_ops[d], far)

    for halo in halos:
        halo.wait_recv()
    for g in range(blocks):
        total = jnp.dot(weights[g * members:(g + 1) * members, :], cand[...], preferred_element_type=F32).astype(BF16)
        for w in range(wedges):
            sums[w, g * block_boxes:(g + 1) * block_boxes, :] = total[w * block_boxes:(w + 1) * block_boxes]
    pulls[7].wait()
    local = jnp.zeros(fine_out.shape, F32)
    for w in range(wedges):
        local = local + jnp.dot(sums[w], fine_ops_v[w], preferred_element_type=F32)
    fine_out[...] = local

    for keep in keeps:
        keep.wait()
    for back in backs:
        back.wait_recv()
    for k in range(1, n_dir):
        scale_copies[k].wait_send()
        row_copies[k].wait_send()
    for sent in backs + halos + ops_copies + [list_copy]:
        sent.wait_send()


def per_device(multipoles, box_scale, fine_list, wedge_index, list_count, fine_ops, phases, coarse_list, coarse_ops):
    n_dir, n_space = lax.axis_size("dir"), lax.axis_size("space")
    boxes, coeffs = multipoles.shape
    group = n_dir * boxes
    half = n_dir // 2
    inside = half * boxes
    dirs, _, terms = coarse_list.shape
    wedges = fine_ops.shape[0]
    list_width = fine_list.shape[1]
    block_boxes = 16
    blocks = boxes // block_boxes
    lists = jnp.transpose(coarse_list, (0, 2, 1))

    hbm = pl.BlockSpec(memory_space=pltpu.HBM)
    members = blocks * block_boxes * wedges
    limit = (20 << 20) + 4 * dirs * inside * group + 2 * members * group
    return pl.pallas_call(
        functools.partial(kernel, n_dir, n_space, boxes, dirs, block_boxes),
        out_shape=(
            jax.ShapeDtypeStruct((boxes, coeffs), F32),
            jax.ShapeDtypeStruct((n_dir * dirs, boxes, coeffs), BF16),
        ),
        in_specs=[hbm] * 9,
        out_specs=(pl.BlockSpec(memory_space=pltpu.VMEM), pl.BlockSpec(memory_space=pl.ANY)),
        scratch_shapes=[
            pltpu.VMEM((group + 2 * boxes, coeffs), BF16),
            pltpu.VMEM((n_dir, 1, boxes), F32),
            pltpu.VMEM((dirs, terms, inside), jnp.int32),
            pltpu.VMEM((dirs, terms, inside), jnp.int32),
            pltpu.VMEM((list_width, boxes), jnp.int32),
            pltpu.VMEM((list_width, boxes), jnp.int32),
            pltpu.VMEM((1, boxes), jnp.int32),
            pltpu.VMEM((2, list_width, LANES), jnp.int32),
            pltpu.VMEM(phases.shape, F32),
            pltpu.VMEM(fine_ops.shape, BF16),
            pltpu.VMEM(coarse_ops.shape, BF16),
            pltpu.VMEM(coarse_ops.shape, BF16),
            pltpu.VMEM((inside, dirs * terms), F32),
            pltpu.VMEM((2 * dirs, inside, group), BF16),
            pltpu.VMEM((members, group + 2 * boxes), BF16),
            pltpu.VMEM((2 * dirs, group, coeffs), BF16),
            pltpu.VMEM((wedges, boxes, coeffs), BF16),
            pltpu.VMEM((2 * dirs, half, boxes, coeffs), BF16),
            pltpu.SemaphoreType.DMA((9,)),
        ] + [pltpu.SemaphoreType.DMA((n_dir,))] * 4 + [pltpu.SemaphoreType.DMA((2,))] * 5
        + [pltpu.SemaphoreType.DMA((2 * dirs, half))] * 2,
        compiler_params=pltpu.CompilerParams(
            collective_id=0, has_side_effects=True, vmem_limit_bytes=limit),
        name="translations",
    )(*[
        pltpu.with_memory_space_constraint(value, pltpu.HBM)
        for value in (
            multipoles, box_scale.reshape(1, boxes), lists, fine_list.T, wedge_index.T, list_count.reshape(1, boxes),
            phases, fine_ops, coarse_ops)
    ])


def solution(mesh):
    return jax.shard_map(
        per_device,
        mesh=mesh,
        in_specs=(
            P(("space", "dir"), None),
            P(("space", "dir")),
            P(("space", "dir"), None),
            P(("space", "dir"), None),
            P(("space", "dir")),
            P(),
            P(),
            P("dir", "space", None),
            P("dir", None, None),
        ),
        out_specs=(P(("space", "dir"), None), P(None, ("space", "dir"), None)),
        check_vma=False,
    )
```

```python
import functools
import math

import jax
import jax.numpy as jnp
from jax import lax
from jax.experimental import pallas as pl
from jax.experimental.pallas import tpu as pltpu
from jax.sharding import PartitionSpec as P

MESH = pl.DeviceIdType.MESH
F32 = jnp.float32
BF16 = jnp.bfloat16
LANES = 128
HALF_TURN_HI = 3.140625
HALF_TURN_LO = 9.67653589793e-4
SINE = (1.0, -0.1666666716337204, 0.008333330973982811, -0.00019840856839437038,
        2.752503405645257e-06, -2.388494557692411e-08)
COSINE = (1.0, -0.5, 0.0416666679084301, -0.0013888884568586946, 2.4801034669508226e-05,
          -2.7524427537174332e-07, 1.9903911852026113e-09)


def horner(terms, x):
    total = jnp.full_like(x, terms[-1])
    for term in terms[-2::-1]:
        total = total * x + term
    return total


def signed_turn(angle):
    turns = jnp.floor(angle * (1.0 / math.pi) + 0.5)
    rest = (angle - turns * HALF_TURN_HI) - turns * HALF_TURN_LO
    halves = turns * 0.5
    sign = 1.0 - 4.0 * (halves - jnp.floor(halves))
    square = rest * rest
    return sign, horner(COSINE, square), horner(SINE, square) * rest


def partner(me, k):
    bit, other = 1, me
    while bit <= k:
        if k & bit:
            other = other + bit * (1 - 2 * ((me // bit) % 2))
        bit *= 2
    return other


def kernel(n_dir, n_space, boxes, dirs, block_boxes, mult, scale, lists, fine_list, wedge_index, list_count, phases,
           fine_ops, coarse_ops,
           fine_out, coarse_out,
           cand, scales, lists_v, far_lists, fine_v, wedge_v, count_v, slots_v, phases_v, fine_ops_v, coarse_ops_v, far_ops,
           columns, counts, weights, turns, rotated, sums, translated, fine_v_out,
           local_sem, rows_send, rows_recv, scale_send, scale_recv, halo_recv, list_sems, ops_send, ops_recv,
           back_sems):
    me = lax.axis_index("dir")
    space = lax.axis_index("space")
    group = n_dir * boxes
    half = n_dir // 2
    inside = half * boxes
    width = mult.shape[1] // 2
    terms = lists.shape[1]
    wedges = fine_ops.shape[0]
    own = pl.ds(pl.multiple_of(me * boxes, boxes), boxes)
    above = lax.rem(space + 1, n_space)
    below = lax.rem(space + n_space - 1, n_space)
    core = lax.rem(space, 2)
    sibling = space + 1 - 2 * core
    far = partner(me, half)
    base = me // half * half
    first_inside = pl.multiple_of(base * boxes, inside)
    first_far = pl.multiple_of((half - base) * boxes, inside)
    share_dirs = dirs // 2
    share = pl.ds(core * share_dirs, share_dirs)

    barrier = pltpu.get_barrier_semaphore()
    for k in range(1, half + 1):
        pl.semaphore_signal(barrier, inc=1, device_id={"dir": partner(me, k)}, device_id_type=MESH)
    for other in (above, below):
        pl.semaphore_signal(barrier, inc=1, device_id={"space": other}, device_id_type=MESH)

    pulls = [
        pltpu.make_async_copy(lists.at[:, :, pl.ds(first_inside, inside)], lists_v, local_sem.at[0]),
        pltpu.make_async_copy(fine_list, fine_v, local_sem.at[1]),
        pltpu.make_async_copy(wedge_index, wedge_v, local_sem.at[2]),
        pltpu.make_async_copy(mult, cand.at[own], local_sem.at[3]),
        pltpu.make_async_copy(scale, scales.at[me], local_sem.at[4]),
        pltpu.make_async_copy(phases, phases_v, local_sem.at[5]),
        pltpu.make_async_copy(coarse_ops, coarse_ops_v, local_sem.at[6]),
        pltpu.make_async_copy(fine_ops, fine_ops_v, local_sem.at[7]),
        pltpu.make_async_copy(list_count, count_v, local_sem.at[8]),
    ]
    for at in (3, 4, 0, 6, 1, 2, 8, 5, 7):
        pulls[at].start()

    def set_columns(values):
        columns[...] = jnp.transpose(
            jnp.concatenate([values[d].astype(F32) for d in range(dirs)], axis=0))

    def set_counts(first_slot):
        def count_rows(i, carry):
            rows = pl.ds(pl.multiple_of(i * boxes, boxes), boxes)
            ids = columns[rows, :]
            lane = lax.broadcasted_iota(jnp.int32, (boxes, group), 1).astype(F32)
            for d in range(dirs):
                total = jnp.zeros((boxes, group), F32)
                for k in range(terms):
                    at = d * terms + k
                    total = total + jnp.where(ids[:, at:at + 1] == lane, 1.0, 0.0)
                counts[first_slot + d, rows, :] = total.astype(BF16)
            return carry

        lax.fori_loop(0, half, count_rows, 0)

    pl.semaphore_wait(barrier, half + 2)

    def rows_of(source):
        return pl.ds(pl.multiple_of(source * boxes, boxes), boxes)

    def stage(k):
        return 0 if k < half else 1 if k == half else 2

    def rows_wait(blocks, sem):
        data = cand.at[pl.ds(0, blocks * boxes)]
        pltpu.make_async_copy(data, data, sem).wait()

    def scales_wait(blocks, sem):
        data = scales.at[pl.ds(0, blocks)]
        pltpu.make_async_copy(data, data, sem).wait()

    def send_rows(k, to, data, source):
        pltpu.make_async_remote_copy(
            data, cand.at[rows_of(source)], rows_send.at[0], rows_recv.at[stage(k)],
            device_id={"dir": partner(me, to)}, device_id_type=MESH).start()

    def send_scale(k, to, data, source):
        pltpu.make_async_remote_copy(
            data, scales.at[source], scale_send.at[0], scale_recv.at[stage(k)],
            device_id={"dir": partner(me, to)}, device_id_type=MESH).start()

    for k in range(half, 0, -1):
        send_scale(k, k, scale, me)
        send_rows(k, k, mult, me)
    for side, other in ((0, above), (1, below)):
        pltpu.make_async_remote_copy(
            mult, cand.at[pl.ds(group + side * boxes, boxes)], rows_send.at[0], halo_recv.at[0],
            device_id={"space": other}, device_id_type=MESH).start()
    list_copy = pltpu.make_async_remote_copy(
        lists.at[:, :, pl.ds(first_far, inside)], far_lists, list_sems.at[0], list_sems.at[1],
        device_id={"dir": far}, device_id_type=MESH)
    list_copy.start()
    pulls[0].wait()
    set_columns(lists_v)
    set_counts(0)

    pulls[1].wait()
    pulls[2].wait()
    pulls[8].wait()
    blocks = boxes // block_boxes
    members = block_boxes * wedges
    width_list = fine_v.shape[0]
    first = fine_v[...] - space * group
    slot_values = jnp.where(
        first < 0, first + (2 * group - me * boxes), jnp.where(first < group, first, first + (boxes - me * boxes)))
    box = lax.broadcasted_iota(jnp.int32, (width_list, boxes), 1)
    term = lax.broadcasted_iota(jnp.int32, (width_list, boxes), 0)
    code_values = jnp.where(term < count_v[...], wedge_v[...] * block_boxes + box % block_boxes, -1)
    packs = LANES // block_boxes
    depth = width_list // packs
    blank = jnp.zeros((width_list, LANES - boxes), jnp.int32)
    slots_v[0] = jnp.concatenate([slot_values, blank], axis=1)
    slots_v[1] = jnp.concatenate([code_values, blank], axis=1)
    pack = lax.broadcasted_iota(jnp.int32, (depth, LANES), 1) // block_boxes

    def cells_of(which, g):
        row = jnp.zeros((depth, LANES), jnp.int32)
        for p in range(packs):
            row = jnp.where(pack == (g + p) % packs, turned[which][p], row)
        if g:
            row = pltpu.roll(row, LANES - g * block_boxes, 1)
        return jnp.concatenate([row[t:t + 1, :] for t in range(depth)], axis=1)

    turned = []
    for which in range(2):
        pieces = [slots_v[which, p * depth:(p + 1) * depth, :] for p in range(packs)]
        turned.append([pieces[0]] + [pltpu.roll(pieces[p], p * block_boxes, 1) for p in range(1, packs)])
    cells = depth * LANES
    for g in range(blocks):
        member = lax.broadcasted_iota(jnp.int32, (members, cells), 0)
        mask = jnp.where(member == cells_of(1, g), 1.0, 0.0).astype(BF16)
        candidate = lax.broadcasted_iota(jnp.int32, (cand.shape[0], cells), 0)
        onehot = jnp.where(candidate == cells_of(0, g), 1.0, 0.0).astype(BF16)
        weights[g * members:(g + 1) * members, :] = lax.dot_general(
            mask, onehot, (((1,), (1,)), ((), ())), preferred_element_type=F32).astype(BF16)

    def angles(source):
        column = jnp.transpose(jnp.broadcast_to(scales[source], (8, boxes)))[:, 0:1]
        for slot in range(2 * dirs):
            owner = me if slot < dirs else far
            angle = phases_v[pl.ds(owner * dirs + slot % dirs, 1), :] * column
            sign, cosine, sine = signed_turn(angle)
            turns[slot, rows_of(source), :width] = cosine * sign
            turns[slot, rows_of(source), width:] = sine * sign

    def rotate(source):
        rows = rows_of(source)
        picked = cand[rows, :].astype(F32)
        real, imag = picked[:, :width], picked[:, width:]
        for slot in range(2 * dirs):
            cosine, sine = turns[slot, rows, :width], turns[slot, rows, width:]
            rotated[slot, rows, :width] = (real * cosine - imag * sine).astype(BF16)
            rotated[slot, rows, width:] = (real * sine + imag * cosine).astype(BF16)

    pulls[3].wait()
    pulls[4].wait()
    pulls[5].wait()
    angles(me)
    rotate(me)
    scales_wait(1, scale_recv.at[1])
    for k in range(half - 1, 0, -1):
        send_scale(half + k, k, scales.at[far], far)
    rows_wait(1, rows_recv.at[1])
    for k in range(half - 1, 0, -1):
        send_rows(half + k, k, cand.at[rows_of(far)], far)
    pulls[6].wait()
    ops_copies = [pltpu.make_async_remote_copy(
        coarse_ops_v.at[share], far_ops.at[share], ops_send.at[0], ops_recv.at[0],
        device_id={"dir": far}, device_id_type=MESH)]
    ops_copies[0].start()

    angles(far)
    scales_wait(half - 1, scale_recv.at[0])
    for k in range(1, half):
        angles(partner(me, k))
    rotate(far)
    rows_wait(half - 1, rows_recv.at[0])
    for k in range(1, half):
        rotate(partner(me, k))
    list_copy.wait_recv()
    set_columns(far_lists)
    set_counts(dirs)
    scales_wait(half - 1, scale_recv.at[2])
    for k in range(half + 1, n_dir):
        angles(partner(me, k))
    rows_wait(half - 1, rows_recv.at[2])
    for k in range(half + 1, n_dir):
        rotate(partner(me, k))

    def translate(slot, d, at, matrix, owner):
        gathered = jnp.dot(counts[at], rotated[at], preferred_element_type=F32).astype(BF16)
        result = jnp.dot(gathered, matrix, preferred_element_type=F32).astype(BF16)
        for member in range(half):
            translated[slot, member] = result[member * boxes:(member + 1) * boxes]
        here = coarse_out.at[owner * dirs + d]
        for k in range(half - 1, 0, -1):
            to = partner(me, k)
            pltpu.make_async_remote_copy(
                translated.at[slot, to - base], here, back_sems.at[0], back_sems.at[1],
                device_id={"dir": to}, device_id_type=MESH).start()
        pltpu.make_async_copy(translated.at[slot, me - base], here, back_sems.at[2]).start()

    for d in range(dirs):
        translate(d, d, d, coarse_ops_v[d], me)
    ops_copies[0].wait_recv()
    ops_copies.append(pltpu.make_async_remote_copy(
        far_ops.at[share], far_ops.at[share], ops_send.at[1], ops_recv.at[1],
        device_id={"space": sibling}, device_id_type=MESH))
    ops_copies[1].start()
    for i in range(share_dirs):
        d = core * share_dirs + i
        translate(dirs + i, d, dirs + d, far_ops[d], far)
    ops_copies[1].wait_recv()
    for i in range(share_dirs):
        d = (1 - core) * share_dirs + i
        translate(dirs + share_dirs + i, d, dirs + d, far_ops[d], far)

    rows_wait(2, halo_recv.at[0])
    for g in range(blocks):
        total = jnp.dot(weights[g * members:(g + 1) * members, :], cand[...], preferred_element_type=F32).astype(BF16)
        for w in range(wedges):
            sums[w, g * block_boxes:(g + 1) * block_boxes, :] = total[w * block_boxes:(w + 1) * block_boxes]
    pulls[7].wait()
    local = jnp.zeros(fine_v_out.shape, F32)
    for w in range(wedges):
        local = local + jnp.dot(sums[w], fine_ops_v[w], preferred_element_type=F32)
    fine_v_out[...] = local
    fine_copy = pltpu.make_async_copy(fine_v_out, fine_out, local_sem.at[0])
    fine_copy.start()

    fine_copy.wait()
    kept = translated.at[:, pl.ds(0, 1)]
    pltpu.make_async_copy(kept, kept, back_sems.at[2]).wait()
    moved = translated.at[:, pl.ds(0, half - 1)]
    pltpu.make_async_copy(moved, moved, back_sems.at[1]).wait()
    pltpu.make_async_copy(moved, moved, back_sems.at[0]).wait()
    rows_wait(n_dir + 1, rows_send.at[0])
    scales_wait(n_dir - 1, scale_send.at[0])
    for sent in ops_copies + [list_copy]:
        sent.wait_send()


def settle(fine_in, coarse_in, fine_out, coarse_out, sems):
    copies = [
        pltpu.make_async_copy(coarse_in, coarse_out, sems.at[0]),
        pltpu.make_async_copy(fine_in, fine_out, sems.at[1]),
    ]
    for copy in copies:
        copy.start()
    for copy in copies:
        copy.wait()


def per_device(multipoles, box_scale, fine_list, wedge_index, list_count, fine_ops, phases, coarse_list, coarse_ops):
    n_dir, n_space = lax.axis_size("dir"), lax.axis_size("space")
    boxes, coeffs = multipoles.shape
    group = n_dir * boxes
    half = n_dir // 2
    inside = half * boxes
    dirs, _, terms = coarse_list.shape
    wedges = fine_ops.shape[0]
    list_width = fine_list.shape[1]
    block_boxes = 16
    blocks = boxes // block_boxes
    lists = jnp.transpose(coarse_list, (0, 2, 1))

    hbm = pl.BlockSpec(memory_space=pltpu.HBM)
    members = blocks * block_boxes * wedges
    limit = (20 << 20) + 4 * dirs * group * (inside + 2 * coeffs) + 2 * members * group
    outs = pl.pallas_call(
        functools.partial(kernel, n_dir, n_space, boxes, dirs, block_boxes),
        out_shape=(
            jax.ShapeDtypeStruct((boxes, coeffs), F32),
            jax.ShapeDtypeStruct((n_dir * dirs, boxes, coeffs), BF16),
        ),
        in_specs=[hbm] * 9,
        out_specs=(pl.BlockSpec(memory_space=pl.ANY), pl.BlockSpec(memory_space=pl.ANY)),
        scratch_shapes=[
            pltpu.VMEM((group + 2 * boxes, coeffs), BF16),
            pltpu.VMEM((n_dir, 1, boxes), F32),
            pltpu.VMEM((dirs, terms, inside), jnp.int32),
            pltpu.VMEM((dirs, terms, inside), jnp.int32),
            pltpu.VMEM((list_width, boxes), jnp.int32),
            pltpu.VMEM((list_width, boxes), jnp.int32),
            pltpu.VMEM((1, boxes), jnp.int32),
            pltpu.VMEM((2, list_width, LANES), jnp.int32),
            pltpu.VMEM(phases.shape, F32),
            pltpu.VMEM(fine_ops.shape, BF16),
            pltpu.VMEM(coarse_ops.shape, BF16),
            pltpu.VMEM(coarse_ops.shape, BF16),
            pltpu.VMEM((inside, dirs * terms), F32),
            pltpu.VMEM((2 * dirs, inside, group), BF16),
            pltpu.VMEM((members, group + 2 * boxes), BF16),
            pltpu.VMEM((2 * dirs, group, coeffs), F32),
            pltpu.VMEM((2 * dirs, group, coeffs), BF16),
            pltpu.VMEM((wedges, boxes, coeffs), BF16),
            pltpu.VMEM((2 * dirs, half, boxes, coeffs), BF16),
            pltpu.VMEM((boxes, coeffs), F32),
            pltpu.SemaphoreType.DMA((9,)),
        ] + [pltpu.SemaphoreType.DMA((n,)) for n in (1, 3, 1, 3, 1, 2, 2, 2, 3)],
        compiler_params=pltpu.CompilerParams(
            collective_id=0, has_side_effects=True, vmem_limit_bytes=limit),
        name="translations",
    )(*[
        pltpu.with_memory_space_constraint(value, pltpu.HBM)
        for value in (
            multipoles, box_scale.reshape(1, boxes), lists, fine_list.T, wedge_index.T, list_count.reshape(1, boxes),
            phases, fine_ops, coarse_ops)
    ])
    return pl.pallas_call(
        settle,
        out_shape=tuple(jax.ShapeDtypeStruct(out.shape, out.dtype) for out in outs),
        in_specs=[pl.BlockSpec(memory_space=pltpu.VMEM)] * 2,
        out_specs=tuple(pl.BlockSpec(memory_space=pltpu.HBM) for _ in outs),
        scratch_shapes=[pltpu.SemaphoreType.DMA((2,))],
        name="settle",
    )(*[pltpu.with_memory_space_constraint(out, pltpu.VMEM) for out in outs])


def solution(mesh):
    return jax.shard_map(
        per_device,
        mesh=mesh,
        in_specs=(
            P(("space", "dir"), None),
            P(("space", "dir")),
            P(("space", "dir"), None),
            P(("space", "dir"), None),
            P(("space", "dir")),
            P(),
            P(),
            P("dir", "space", None),
            P("dir", None, None),
        ),
        out_specs=(P(("space", "dir"), None), P(None, ("space", "dir"), None)),
        check_vma=False,
    )
```

```python
import functools
import math

import jax
import jax.numpy as jnp
from jax import lax
from jax.experimental import pallas as pl
from jax.experimental.pallas import tpu as pltpu
from jax.sharding import PartitionSpec as P

MESH = pl.DeviceIdType.MESH
F32 = jnp.float32
BF16 = jnp.bfloat16
LANES = 128
HALF_TURN_HI = 3.140625
HALF_TURN_LO = 9.67653589793e-4
SINE = (1.0, -0.1666666716337204, 0.008333330973982811, -0.00019840856839437038,
        2.752503405645257e-06, -2.388494557692411e-08)
COSINE = (1.0, -0.5, 0.0416666679084301, -0.0013888884568586946, 2.4801034669508226e-05,
          -2.7524427537174332e-07, 1.9903911852026113e-09)


def horner(terms, x):
    total = jnp.full_like(x, terms[-1])
    for term in terms[-2::-1]:
        total = total * x + term
    return total


def signed_turn(angle):
    turns = jnp.floor(angle * (1.0 / math.pi) + 0.5)
    rest = (angle - turns * HALF_TURN_HI) - turns * HALF_TURN_LO
    halves = turns * 0.5
    sign = 1.0 - 4.0 * (halves - jnp.floor(halves))
    square = rest * rest
    return sign, horner(COSINE, square), horner(SINE, square) * rest


def partner(me, k):
    bit, other = 1, me
    while bit <= k:
        if k & bit:
            other = other + bit * (1 - 2 * ((me // bit) % 2))
        bit *= 2
    return other


def kernel(n_dir, n_space, boxes, dirs, block_boxes, mult, scale, lists, fine_list, wedge_index, list_count, phases,
           fine_ops, coarse_ops,
           fine_out, coarse_out,
           cand, scales, lists_v, far_lists, fine_v, wedge_v, count_v, slots_v, phases_v, fine_ops_v, coarse_ops_v, far_ops,
           columns, counts, weights, turns, rotated, sums, translated, gathered_out, gathered_in, fine_v_out,
           local_sem, rows_send, rows_recv, scale_send, scale_recv, halo_recv, list_sems, ops_sems,
           swap_sems, back_sems):
    me = lax.axis_index("dir")
    space = lax.axis_index("space")
    group = n_dir * boxes
    half = n_dir // 2
    inside = half * boxes
    width = mult.shape[1] // 2
    terms = lists.shape[1]
    wedges = fine_ops.shape[0]
    own = pl.ds(pl.multiple_of(me * boxes, boxes), boxes)
    above = lax.rem(space + 1, n_space)
    below = lax.rem(space + n_space - 1, n_space)
    core = lax.rem(space, 2)
    sibling = space + 1 - 2 * core
    far = partner(me, half)
    base = me // half * half
    first_inside = pl.multiple_of(base * boxes, inside)
    first_far = pl.multiple_of((half - base) * boxes, inside)
    share_dirs = dirs // 2
    level = space // 2
    levels = n_space // 2
    deep = coarse_ops.shape[1] // levels
    storeys = [2 * lax.rem(level + i, levels) + core for i in range(1, levels)]
    share = pl.ds(core * share_dirs, share_dirs)

    barrier = pltpu.get_barrier_semaphore()
    for k in range(1, half + 1):
        pl.semaphore_signal(barrier, inc=1, device_id={"dir": partner(me, k)}, device_id_type=MESH)
    for k in range(1, half):
        pl.semaphore_signal(
            barrier, inc=1, device_id={"dir": partner(me, k), "space": sibling}, device_id_type=MESH)
    for other in [above, below] + storeys:
        pl.semaphore_signal(barrier, inc=1, device_id={"space": other}, device_id_type=MESH)

    pulls = [
        pltpu.make_async_copy(lists.at[:, :, pl.ds(first_inside, inside)], lists_v, local_sem.at[0]),
        pltpu.make_async_copy(fine_list, fine_v, local_sem.at[1]),
        pltpu.make_async_copy(wedge_index, wedge_v, local_sem.at[2]),
        pltpu.make_async_copy(mult, cand.at[own], local_sem.at[3]),
        pltpu.make_async_copy(scale, scales.at[me], local_sem.at[4]),
        pltpu.make_async_copy(phases, phases_v, local_sem.at[5]),
        pltpu.make_async_copy(coarse_ops, coarse_ops_v, local_sem.at[6]),
        pltpu.make_async_copy(fine_ops, fine_ops_v, local_sem.at[7]),
        pltpu.make_async_copy(list_count, count_v, local_sem.at[8]),
    ]
    for at in (3, 4, 0, 6, 1, 2, 8, 5, 7):
        pulls[at].start()

    def set_columns(values):
        columns[...] = jnp.transpose(
            jnp.concatenate([values[d].astype(F32) for d in range(dirs)], axis=0))

    def set_counts(first_slot):
        def count_rows(i, carry):
            rows = pl.ds(pl.multiple_of(i * boxes, boxes), boxes)
            ids = columns[rows, :]
            lane = lax.broadcasted_iota(jnp.int32, (boxes, group), 1).astype(F32)
            for d in range(dirs):
                total = jnp.zeros((boxes, group), F32)
                for k in range(terms):
                    at = d * terms + k
                    total = total + jnp.where(ids[:, at:at + 1] == lane, 1.0, 0.0)
                counts[first_slot + d, rows, :] = total.astype(BF16)
            return carry

        lax.fori_loop(0, half, count_rows, 0)

    pl.semaphore_wait(barrier, 2 * half + levels)

    def rows_of(source):
        return pl.ds(pl.multiple_of(source * boxes, boxes), boxes)

    def stage(k):
        return 0 if k < half else 1 if k == half else 2

    def rows_wait(blocks, sem):
        data = cand.at[pl.ds(0, blocks * boxes)]
        pltpu.make_async_copy(data, data, sem).wait()

    def scales_wait(blocks, sem):
        data = scales.at[pl.ds(0, blocks)]
        pltpu.make_async_copy(data, data, sem).wait()

    def send_rows(k, to, data, source):
        pltpu.make_async_remote_copy(
            data, cand.at[rows_of(source)], rows_send.at[0], rows_recv.at[stage(k)],
            device_id={"dir": partner(me, to)}, device_id_type=MESH).start()

    def send_scale(k, to, data, source):
        pltpu.make_async_remote_copy(
            data, scales.at[source], scale_send.at[0], scale_recv.at[stage(k)],
            device_id={"dir": partner(me, to)}, device_id_type=MESH).start()

    for k in range(half, 0, -1):
        send_scale(k, k, scale, me)
        send_rows(k, k, mult, me)
    for side, other in ((0, above), (1, below)):
        pltpu.make_async_remote_copy(
            mult, cand.at[pl.ds(group + side * boxes, boxes)], rows_send.at[0], halo_recv.at[0],
            device_id={"space": other}, device_id_type=MESH).start()
    list_copy = pltpu.make_async_remote_copy(
        lists.at[:, :, pl.ds(first_far, inside)], far_lists, list_sems.at[0], list_sems.at[1],
        device_id={"dir": far}, device_id_type=MESH)
    list_copy.start()
    deeps = pl.ds(pl.multiple_of(level * deep, deep), deep)
    ops_copy = pltpu.make_async_remote_copy(
        coarse_ops_v.at[share, deeps], far_ops.at[:, deeps], ops_sems.at[0], ops_sems.at[1],
        device_id={"dir": far}, device_id_type=MESH)

    pulls[0].wait()
    set_columns(lists_v)
    set_counts(0)
    pulls[6].wait()

    pulls[1].wait()
    pulls[2].wait()
    pulls[8].wait()
    blocks = boxes // block_boxes
    members = block_boxes * wedges
    width_list = fine_v.shape[0]
    first = fine_v[...] - space * group
    slot_values = jnp.where(
        first < 0, first + (2 * group - me * boxes), jnp.where(first < group, first, first + (boxes - me * boxes)))
    box = lax.broadcasted_iota(jnp.int32, (width_list, boxes), 1)
    term = lax.broadcasted_iota(jnp.int32, (width_list, boxes), 0)
    code_values = jnp.where(term < count_v[...], wedge_v[...] * block_boxes + box % block_boxes, -1)
    packs = LANES // block_boxes
    depth = width_list // packs
    blank = jnp.zeros((width_list, LANES - boxes), jnp.int32)
    slots_v[0] = jnp.concatenate([slot_values, blank], axis=1)
    slots_v[1] = jnp.concatenate([code_values, blank], axis=1)
    pack = lax.broadcasted_iota(jnp.int32, (depth, LANES), 1) // block_boxes

    def cells_of(which, g):
        row = jnp.zeros((depth, LANES), jnp.int32)
        for p in range(packs):
            row = jnp.where(pack == (g + p) % packs, turned[which][p], row)
        if g:
            row = pltpu.roll(row, LANES - g * block_boxes, 1)
        return jnp.concatenate([row[t:t + 1, :] for t in range(depth)], axis=1)

    turned = []
    for which in range(2):
        pieces = [slots_v[which, p * depth:(p + 1) * depth, :] for p in range(packs)]
        turned.append([pieces[0]] + [pltpu.roll(pieces[p], p * block_boxes, 1) for p in range(1, packs)])
    cells = depth * LANES
    for g in range(blocks):
        member = lax.broadcasted_iota(jnp.int32, (members, cells), 0)
        mask = jnp.where(member == cells_of(1, g), 1.0, 0.0).astype(BF16)
        candidate = lax.broadcasted_iota(jnp.int32, (cand.shape[0], cells), 0)
        onehot = jnp.where(candidate == cells_of(0, g), 1.0, 0.0).astype(BF16)
        weights[g * members:(g + 1) * members, :] = lax.dot_general(
            mask, onehot, (((1,), (1,)), ((), ())), preferred_element_type=F32).astype(BF16)
        if g == 1:
            ops_copy.start()

    def angles(source):
        column = jnp.transpose(jnp.broadcast_to(scales[source], (8, boxes)))[:, 0:1]
        for slot in range(2 * dirs):
            owner = me if slot < dirs else far
            angle = phases_v[pl.ds(owner * dirs + slot % dirs, 1), :] * column
            sign, cosine, sine = signed_turn(angle)
            turns[slot, rows_of(source), :width] = cosine * sign
            turns[slot, rows_of(source), width:] = sine * sign

    def rotate(source):
        rows = rows_of(source)
        picked = cand[rows, :].astype(F32)
        real, imag = picked[:, :width], picked[:, width:]
        for slot in range(2 * dirs):
            cosine, sine = turns[slot, rows, :width], turns[slot, rows, width:]
            rotated[slot, rows, :width] = (real * cosine - imag * sine).astype(BF16)
            rotated[slot, rows, width:] = (real * sine + imag * cosine).astype(BF16)

    pulls[3].wait()
    pulls[4].wait()
    pulls[5].wait()
    angles(me)
    rotate(me)
    scales_wait(1, scale_recv.at[1])
    for k in range(half - 1, 0, -1):
        send_scale(half + k, k, scales.at[far], far)
    rows_wait(1, rows_recv.at[1])
    for k in range(half - 1, 0, -1):
        send_rows(half + k, k, cand.at[rows_of(far)], far)
    angles(far)
    scales_wait(half - 1, scale_recv.at[0])
    for k in range(1, half):
        angles(partner(me, k))
    rotate(far)
    rows_wait(half - 1, rows_recv.at[0])
    for k in range(1, half):
        rotate(partner(me, k))
    list_copy.wait_recv()
    set_columns(far_lists)
    set_counts(dirs)
    ops_copy.wait_recv()
    for other in storeys:
        pltpu.make_async_remote_copy(
            far_ops.at[:, deeps], far_ops.at[:, deeps], ops_sems.at[2], ops_sems.at[3],
            device_id={"space": other}, device_id_type=MESH).start()
    scales_wait(half - 1, scale_recv.at[2])
    for k in range(half + 1, n_dir):
        angles(partner(me, k))
    rows_wait(half - 1, rows_recv.at[2])
    for k in range(half + 1, n_dir):
        rotate(partner(me, k))

    def gather(at):
        return jnp.dot(counts[at], rotated[at], preferred_element_type=F32).astype(BF16)

    def translate(gathered, matrix, slot, here, home):
        result = jnp.dot(gathered, matrix, preferred_element_type=F32).astype(BF16)
        first = slot * half
        for member in range(half):
            translated[first + member] = result[member * boxes:(member + 1) * boxes]
        for k in range(half - 1, -1, -1):
            to = partner(me, k)
            piece = translated.at[first + to - base]
            if k or not home:
                where = {"dir": to} if home else {"dir": to, "space": sibling}
                pltpu.make_async_remote_copy(
                    piece, here, back_sems.at[0], back_sems.at[1], device_id=where, device_id_type=MESH).start()
            else:
                pltpu.make_async_copy(piece, here, back_sems.at[2]).start()

    def far_out(i):
        return coarse_out.at[far * dirs + core * share_dirs + i]

    for d in range(dirs):
        translate(gather(d), coarse_ops_v[d], d, coarse_out.at[me * dirs + d], True)
        if d == 0:
            for i in range(share_dirs):
                gathered_out[i] = gather(dirs + (1 - core) * share_dirs + i)
            swap = pltpu.make_async_remote_copy(
                gathered_out, gathered_in, swap_sems.at[0], swap_sems.at[1],
                device_id={"space": sibling}, device_id_type=MESH)
            swap.start()
    own_gathered = [gather(dirs + core * share_dirs + i) for i in range(share_dirs)]
    rest = far_ops.at[:, pl.ds(0, (levels - 1) * deep)]
    pltpu.make_async_copy(rest, rest, ops_sems.at[3]).wait()
    for i in range(share_dirs):
        translate(own_gathered[i], far_ops[i], dirs + i, far_out(i), True)
    swap.wait_recv()
    for i in range(share_dirs):
        translate(gathered_in[i], far_ops[i], dirs + share_dirs + i, far_out(i), False)

    rows_wait(2, halo_recv.at[0])
    for g in range(blocks):
        total = jnp.dot(weights[g * members:(g + 1) * members, :], cand[...], preferred_element_type=F32).astype(BF16)
        for w in range(wedges):
            sums[w, g * block_boxes:(g + 1) * block_boxes, :] = total[w * block_boxes:(w + 1) * block_boxes]
    pulls[7].wait()
    local = jnp.zeros(fine_v_out.shape, F32)
    for w in range(wedges):
        local = local + jnp.dot(sums[w], fine_ops_v[w], preferred_element_type=F32)
    fine_v_out[...] = local
    fine_copy = pltpu.make_async_copy(fine_v_out, fine_out, local_sem.at[0])
    fine_copy.start()

    fine_copy.wait()
    kept = translated.at[pl.ds(0, dirs + share_dirs)]
    pltpu.make_async_copy(kept, kept, back_sems.at[2]).wait()
    moved = translated.at[pl.ds(0, 2 * dirs * half - dirs - share_dirs)]
    pltpu.make_async_copy(moved, moved, back_sems.at[1]).wait()
    pltpu.make_async_copy(moved, moved, back_sems.at[0]).wait()
    rows_wait(n_dir + 1, rows_send.at[0])
    scales_wait(n_dir - 1, scale_send.at[0])
    pltpu.make_async_copy(rest, rest, ops_sems.at[2]).wait()
    for sent in (ops_copy, list_copy, swap):
        sent.wait_send()


def settle(fine_in, coarse_in, fine_out, coarse_out, sems):
    copies = [
        pltpu.make_async_copy(coarse_in, coarse_out, sems.at[0]),
        pltpu.make_async_copy(fine_in, fine_out, sems.at[1]),
    ]
    for copy in copies:
        copy.start()
    for copy in copies:
        copy.wait()


def per_device(multipoles, box_scale, fine_list, wedge_index, list_count, fine_ops, phases, coarse_list, coarse_ops):
    n_dir, n_space = lax.axis_size("dir"), lax.axis_size("space")
    boxes, coeffs = multipoles.shape
    group = n_dir * boxes
    half = n_dir // 2
    inside = half * boxes
    dirs, _, terms = coarse_list.shape
    wedges = fine_ops.shape[0]
    list_width = fine_list.shape[1]
    block_boxes = 16
    blocks = boxes // block_boxes
    lists = jnp.transpose(coarse_list, (0, 2, 1))

    hbm = pl.BlockSpec(memory_space=pltpu.HBM)
    members = blocks * block_boxes * wedges
    limit = (20 << 20) + 4 * dirs * group * (inside + 2 * coeffs) + 2 * members * group
    outs = pl.pallas_call(
        functools.partial(kernel, n_dir, n_space, boxes, dirs, block_boxes),
        out_shape=(
            jax.ShapeDtypeStruct((boxes, coeffs), F32),
            jax.ShapeDtypeStruct((n_dir * dirs, boxes, coeffs), BF16),
        ),
        in_specs=[hbm] * 9,
        out_specs=(pl.BlockSpec(memory_space=pl.ANY), pl.BlockSpec(memory_space=pl.ANY)),
        scratch_shapes=[
            pltpu.VMEM((group + 2 * boxes, coeffs), BF16),
            pltpu.VMEM((n_dir, 1, boxes), F32),
            pltpu.VMEM((dirs, terms, inside), jnp.int32),
            pltpu.VMEM((dirs, terms, inside), jnp.int32),
            pltpu.VMEM((list_width, boxes), jnp.int32),
            pltpu.VMEM((list_width, boxes), jnp.int32),
            pltpu.VMEM((1, boxes), jnp.int32),
            pltpu.VMEM((2, list_width, LANES), jnp.int32),
            pltpu.VMEM(phases.shape, F32),
            pltpu.VMEM(fine_ops.shape, BF16),
            pltpu.VMEM(coarse_ops.shape, BF16),
            pltpu.VMEM((dirs // 2,) + coarse_ops.shape[1:], BF16),
            pltpu.VMEM((inside, dirs * terms), F32),
            pltpu.VMEM((2 * dirs, inside, group), BF16),
            pltpu.VMEM((members, group + 2 * boxes), BF16),
            pltpu.VMEM((2 * dirs, group, coeffs), F32),
            pltpu.VMEM((2 * dirs, group, coeffs), BF16),
            pltpu.VMEM((wedges, boxes, coeffs), BF16),
            pltpu.VMEM((2 * dirs * half, boxes, coeffs), BF16),
            pltpu.VMEM((dirs // 2, inside, coeffs), BF16),
            pltpu.VMEM((dirs // 2, inside, coeffs), BF16),
            pltpu.VMEM((boxes, coeffs), F32),
            pltpu.SemaphoreType.DMA((9,)),
        ] + [pltpu.SemaphoreType.DMA((n,)) for n in (1, 3, 1, 3, 1, 2, 4, 2, 3)],
        compiler_params=pltpu.CompilerParams(
            collective_id=0, has_side_effects=True, vmem_limit_bytes=limit),
        name="translations",
    )(*[
        pltpu.with_memory_space_constraint(value, pltpu.HBM)
        for value in (
            multipoles, box_scale.reshape(1, boxes), lists, fine_list.T, wedge_index.T, list_count.reshape(1, boxes),
            phases, fine_ops, coarse_ops)
    ])
    return pl.pallas_call(
        settle,
        out_shape=tuple(jax.ShapeDtypeStruct(out.shape, out.dtype) for out in outs),
        in_specs=[pl.BlockSpec(memory_space=pltpu.VMEM)] * 2,
        out_specs=tuple(pl.BlockSpec(memory_space=pltpu.HBM) for _ in outs),
        scratch_shapes=[pltpu.SemaphoreType.DMA((2,))],
        name="settle",
    )(*[pltpu.with_memory_space_constraint(out, pltpu.VMEM) for out in outs])


def solution(mesh):
    return jax.shard_map(
        per_device,
        mesh=mesh,
        in_specs=(
            P(("space", "dir"), None),
            P(("space", "dir")),
            P(("space", "dir"), None),
            P(("space", "dir"), None),
            P(("space", "dir")),
            P(),
            P(),
            P("dir", "space", None),
            P("dir", None, None),
        ),
        out_specs=(P(("space", "dir"), None), P(None, ("space", "dir"), None)),
        check_vma=False,
    )
```

```python
import functools
import math

import jax
import jax.numpy as jnp
from jax import lax
from jax.experimental import pallas as pl
from jax.experimental.pallas import tpu as pltpu
from jax.sharding import PartitionSpec as P

MESH = pl.DeviceIdType.MESH
F32 = jnp.float32
BF16 = jnp.bfloat16
LANES = 128
HALF_TURN_HI = 3.140625
HALF_TURN_LO = 9.67653589793e-4
SINE = (1.0, -0.1666666716337204, 0.008333330973982811, -0.00019840856839437038,
        2.752503405645257e-06, -2.388494557692411e-08)
COSINE = (1.0, -0.5, 0.0416666679084301, -0.0013888884568586946, 2.4801034669508226e-05,
          -2.7524427537174332e-07, 1.9903911852026113e-09)


def horner(terms, x):
    total = jnp.full_like(x, terms[-1])
    for term in terms[-2::-1]:
        total = total * x + term
    return total


def signed_turn(angle):
    turns = jnp.floor(angle * (1.0 / math.pi) + 0.5)
    rest = (angle - turns * HALF_TURN_HI) - turns * HALF_TURN_LO
    halves = turns * 0.5
    sign = 1.0 - 4.0 * (halves - jnp.floor(halves))
    square = rest * rest
    return sign, horner(COSINE, square), horner(SINE, square) * rest


def partner(me, k):
    bit, other = 1, me
    while bit <= k:
        if k & bit:
            other = other + bit * (1 - 2 * ((me // bit) % 2))
        bit *= 2
    return other


def kernel(n_dir, n_space, boxes, dirs, block_boxes, mult, scale, lists, fine_list, wedge_index, list_count, phases,
           fine_ops, coarse_ops,
           fine_out, coarse_out,
           cand, scales, lists_v, far_lists, fine_v, wedge_v, count_v, slots_v, phases_v, fine_ops_v, coarse_ops_v, far_ops,
           columns, counts, weights, turns, rotated, sums, translated, gathered_out, gathered_in, fine_v_out,
           local_sem, rows_send, rows_recv, scale_send, scale_recv, halo_recv, list_sems, ops_sems,
           swap_sems, back_sems):
    me = lax.axis_index("dir")
    space = lax.axis_index("space")
    group = n_dir * boxes
    half = n_dir // 2
    inside = half * boxes
    width = mult.shape[1] // 2
    terms = lists.shape[1]
    wedges = fine_ops.shape[0]
    own = pl.ds(pl.multiple_of(me * boxes, boxes), boxes)
    above = lax.rem(space + 1, n_space)
    below = lax.rem(space + n_space - 1, n_space)
    core = lax.rem(space, 2)
    sibling = space + 1 - 2 * core
    far = partner(me, half)
    base = me // half * half
    first_inside = pl.multiple_of(base * boxes, inside)
    first_far = pl.multiple_of((half - base) * boxes, inside)
    share_dirs = dirs // 2
    level = space // 2
    levels = n_space // 2
    shared_deep = coarse_ops.shape[1] // 2
    deep = shared_deep // levels
    passed = pl.ds(pl.multiple_of(level * deep, deep), deep)
    common = pl.ds(shared_deep, coarse_ops.shape[1] - shared_deep)
    storeys = [2 * lax.rem(level + i, levels) + core for i in range(1, levels)]
    share = pl.ds(core * share_dirs, share_dirs)

    barrier = pltpu.get_barrier_semaphore()
    for k in range(1, half + 1):
        pl.semaphore_signal(barrier, inc=1, device_id={"dir": partner(me, k)}, device_id_type=MESH)
    for k in range(1, half):
        pl.semaphore_signal(
            barrier, inc=1, device_id={"dir": partner(me, k), "space": sibling}, device_id_type=MESH)
    for other in [above, below] + storeys:
        pl.semaphore_signal(barrier, inc=1, device_id={"space": other}, device_id_type=MESH)

    pulls = [
        pltpu.make_async_copy(lists.at[:, :, pl.ds(first_inside, inside)], lists_v, local_sem.at[0]),
        pltpu.make_async_copy(fine_list, fine_v, local_sem.at[1]),
        pltpu.make_async_copy(wedge_index, wedge_v, local_sem.at[2]),
        pltpu.make_async_copy(mult, cand.at[own], local_sem.at[3]),
        pltpu.make_async_copy(scale, scales.at[me], local_sem.at[4]),
        pltpu.make_async_copy(phases, phases_v, local_sem.at[5]),
        pltpu.make_async_copy(coarse_ops, coarse_ops_v, local_sem.at[6]),
        pltpu.make_async_copy(fine_ops, fine_ops_v, local_sem.at[7]),
        pltpu.make_async_copy(list_count, count_v, local_sem.at[8]),
    ]
    for at in (3, 4, 0, 6, 1, 2, 8, 5, 7):
        pulls[at].start()

    def set_columns(values):
        columns[...] = jnp.transpose(
            jnp.concatenate([values[d].astype(F32) for d in range(dirs)], axis=0))

    def set_counts(first_slot):
        def count_rows(i, carry):
            rows = pl.ds(pl.multiple_of(i * boxes, boxes), boxes)
            ids = columns[rows, :]
            lane = lax.broadcasted_iota(jnp.int32, (boxes, group), 1).astype(F32)
            for d in range(dirs):
                total = jnp.zeros((boxes, group), F32)
                for k in range(terms):
                    at = d * terms + k
                    total = total + jnp.where(ids[:, at:at + 1] == lane, 1.0, 0.0)
                counts[first_slot + d, rows, :] = total.astype(BF16)
            return carry

        lax.fori_loop(0, half, count_rows, 0)

    pl.semaphore_wait(barrier, 2 * half + levels)

    def rows_of(source):
        return pl.ds(pl.multiple_of(source * boxes, boxes), boxes)

    def stage(k):
        return 0 if k < half else 1 if k == half else 2

    def rows_wait(blocks, sem):
        data = cand.at[pl.ds(0, blocks * boxes)]
        pltpu.make_async_copy(data, data, sem).wait()

    def scales_wait(blocks, sem):
        data = scales.at[pl.ds(0, blocks)]
        pltpu.make_async_copy(data, data, sem).wait()

    def send_rows(k, to, data, source):
        pltpu.make_async_remote_copy(
            data, cand.at[rows_of(source)], rows_send.at[0], rows_recv.at[stage(k)],
            device_id={"dir": partner(me, to)}, device_id_type=MESH).start()

    def send_scale(k, to, data, source):
        pltpu.make_async_remote_copy(
            data, scales.at[source], scale_send.at[0], scale_recv.at[stage(k)],
            device_id={"dir": partner(me, to)}, device_id_type=MESH).start()

    pulls[3].wait()
    pulls[4].wait()
    for k in range(half, 0, -1):
        send_scale(k, k, scales.at[me], me)
        send_rows(k, k, cand.at[own], me)
    for side, other in ((0, above), (1, below)):
        pltpu.make_async_remote_copy(
            mult, cand.at[pl.ds(group + side * boxes, boxes)], rows_send.at[0], halo_recv.at[0],
            device_id={"space": other}, device_id_type=MESH).start()
    list_copy = pltpu.make_async_remote_copy(
        lists.at[:, :, pl.ds(first_far, inside)], far_lists, list_sems.at[0], list_sems.at[1],
        device_id={"dir": far}, device_id_type=MESH)
    list_copy.start()
    ops_copies = [pltpu.make_async_remote_copy(
        coarse_ops_v.at[share, rows], far_ops.at[:, rows],
        ops_sems.at[0], ops_sems.at[3 + at], device_id={"dir": far}, device_id_type=MESH)
        for at, rows in enumerate((passed, common))]

    pulls[0].wait()
    set_columns(lists_v)
    set_counts(0)
    pulls[6].wait()

    pulls[1].wait()
    pulls[2].wait()
    pulls[8].wait()
    blocks = boxes // block_boxes
    members = block_boxes * wedges
    width_list = fine_v.shape[0]
    first = fine_v[...] - space * group
    slot_values = jnp.where(
        first < 0, first + (2 * group - me * boxes), jnp.where(first < group, first, first + (boxes - me * boxes)))
    box = lax.broadcasted_iota(jnp.int32, (width_list, boxes), 1)
    term = lax.broadcasted_iota(jnp.int32, (width_list, boxes), 0)
    code_values = jnp.where(term < count_v[...], wedge_v[...] * block_boxes + box % block_boxes, -1)
    packs = LANES // block_boxes
    depth = width_list // packs
    blank = jnp.zeros((width_list, LANES - boxes), jnp.int32)
    slots_v[0] = jnp.concatenate([slot_values, blank], axis=1)
    slots_v[1] = jnp.concatenate([code_values, blank], axis=1)
    pack = lax.broadcasted_iota(jnp.int32, (depth, LANES), 1) // block_boxes

    def cells_of(which, g):
        row = jnp.zeros((depth, LANES), jnp.int32)
        for p in range(packs):
            row = jnp.where(pack == (g + p) % packs, turned[which][p], row)
        if g:
            row = pltpu.roll(row, LANES - g * block_boxes, 1)
        return jnp.concatenate([row[t:t + 1, :] for t in range(depth)], axis=1)

    turned = []
    for which in range(2):
        pieces = [slots_v[which, p * depth:(p + 1) * depth, :] for p in range(packs)]
        turned.append([pieces[0]] + [pltpu.roll(pieces[p], p * block_boxes, 1) for p in range(1, packs)])
    cells = depth * LANES
    for g in range(blocks):
        member = lax.broadcasted_iota(jnp.int32, (members, cells), 0)
        mask = jnp.where(member == cells_of(1, g), 1.0, 0.0).astype(BF16)
        candidate = lax.broadcasted_iota(jnp.int32, (cand.shape[0], cells), 0)
        onehot = jnp.where(candidate == cells_of(0, g), 1.0, 0.0).astype(BF16)
        weights[g * members:(g + 1) * members, :] = lax.dot_general(
            mask, onehot, (((1,), (1,)), ((), ())), preferred_element_type=F32).astype(BF16)
        if g == 1:
            for copy in ops_copies:
                copy.start()

    def angles(source):
        column = jnp.transpose(jnp.broadcast_to(scales[source], (8, boxes)))[:, 0:1]
        for slot in range(2 * dirs):
            owner = me if slot < dirs else far
            angle = phases_v[pl.ds(owner * dirs + slot % dirs, 1), :] * column
            sign, cosine, sine = signed_turn(angle)
            turns[slot, rows_of(source), :width] = cosine * sign
            turns[slot, rows_of(source), width:] = sine * sign

    def rotate(source):
        rows = rows_of(source)
        picked = cand[rows, :].astype(F32)
        real, imag = picked[:, :width], picked[:, width:]
        for slot in range(2 * dirs):
            cosine, sine = turns[slot, rows, :width], turns[slot, rows, width:]
            rotated[slot, rows, :width] = (real * cosine - imag * sine).astype(BF16)
            rotated[slot, rows, width:] = (real * sine + imag * cosine).astype(BF16)

    pulls[5].wait()
    angles(me)
    rotate(me)
    scales_wait(1, scale_recv.at[1])
    for k in range(half - 1, 0, -1):
        send_scale(half + k, k, scales.at[far], far)
    rows_wait(1, rows_recv.at[1])
    for k in range(half - 1, 0, -1):
        send_rows(half + k, k, cand.at[rows_of(far)], far)
    angles(far)
    scales_wait(half - 1, scale_recv.at[0])
    for k in range(1, half):
        angles(partner(me, k))
    rotate(far)
    rows_wait(half - 1, rows_recv.at[0])
    for k in range(1, half):
        rotate(partner(me, k))
    list_copy.wait_recv()
    set_columns(far_lists)
    set_counts(dirs)
    scales_wait(half - 1, scale_recv.at[2])
    for k in range(half + 1, n_dir):
        angles(partner(me, k))
    ops_copies[0].wait_recv()
    for other in storeys:
        pltpu.make_async_remote_copy(
            far_ops.at[:, passed], far_ops.at[:, passed], ops_sems.at[1], ops_sems.at[2],
            device_id={"space": other}, device_id_type=MESH).start()
    rows_wait(half - 1, rows_recv.at[2])
    for k in range(half + 1, n_dir):
        rotate(partner(me, k))

    def gather(at):
        return jnp.dot(counts[at], rotated[at], preferred_element_type=F32).astype(BF16)

    def translate(gathered, matrix, slot, here, home):
        result = jnp.dot(gathered, matrix, preferred_element_type=F32).astype(BF16)
        first = slot * half
        for member in range(half):
            translated[first + member] = result[member * boxes:(member + 1) * boxes]
        for k in range(half - 1, -1, -1):
            to = partner(me, k)
            piece = translated.at[first + to - base]
            if k or not home:
                where = {"dir": to} if home else {"dir": to, "space": sibling}
                pltpu.make_async_remote_copy(
                    piece, here, back_sems.at[0], back_sems.at[1], device_id=where, device_id_type=MESH).start()
            else:
                pltpu.make_async_copy(piece, here, back_sems.at[2]).start()

    def far_out(i):
        return coarse_out.at[far * dirs + core * share_dirs + i]

    for d in range(dirs):
        translate(gather(d), coarse_ops_v[d], d, coarse_out.at[me * dirs + d], True)
    for i in range(share_dirs):
        gathered_out[i] = gather(dirs + (1 - core) * share_dirs + i)
    swap = pltpu.make_async_remote_copy(
        gathered_out, gathered_in, swap_sems.at[0], swap_sems.at[1],
        device_id={"space": sibling}, device_id_type=MESH)
    swap.start()
    own_gathered = [gather(dirs + core * share_dirs + i) for i in range(share_dirs)]
    rest = far_ops.at[:, pl.ds(0, (levels - 1) * deep)]
    pltpu.make_async_copy(rest, rest, ops_sems.at[2]).wait()
    ops_copies[1].wait_recv()
    for i in range(share_dirs):
        translate(own_gathered[i], far_ops[i], dirs + i, far_out(i), True)
    swap.wait_recv()
    for i in range(share_dirs):
        translate(gathered_in[i], far_ops[i], dirs + share_dirs + i, far_out(i), False)

    rows_wait(2, halo_recv.at[0])
    for g in range(blocks):
        total = jnp.dot(weights[g * members:(g + 1) * members, :], cand[...], preferred_element_type=F32).astype(BF16)
        for w in range(wedges):
            sums[w, g * block_boxes:(g + 1) * block_boxes, :] = total[w * block_boxes:(w + 1) * block_boxes]
    pulls[7].wait()
    local = jnp.zeros(fine_v_out.shape, F32)
    for w in range(wedges):
        local = local + jnp.dot(sums[w], fine_ops_v[w], preferred_element_type=F32)
    fine_v_out[...] = local
    fine_copy = pltpu.make_async_copy(fine_v_out, fine_out, local_sem.at[0])
    fine_copy.start()

    fine_copy.wait()
    kept = translated.at[pl.ds(0, dirs + share_dirs)]
    pltpu.make_async_copy(kept, kept, back_sems.at[2]).wait()
    moved = translated.at[pl.ds(0, 2 * dirs * half - dirs - share_dirs)]
    pltpu.make_async_copy(moved, moved, back_sems.at[1]).wait()
    pltpu.make_async_copy(moved, moved, back_sems.at[0]).wait()
    rows_wait(n_dir + 1, rows_send.at[0])
    scales_wait(n_dir - 1, scale_send.at[0])
    pltpu.make_async_copy(rest, rest, ops_sems.at[1]).wait()
    mine = far_ops.at[:, pl.ds(0, deep + coarse_ops.shape[1] - shared_deep)]
    pltpu.make_async_copy(mine, mine, ops_sems.at[0]).wait()
    for sent in (list_copy, swap):
        sent.wait_send()


def settle(fine_in, coarse_in, fine_out, coarse_out, sems):
    copies = [
        pltpu.make_async_copy(coarse_in, coarse_out, sems.at[0]),
        pltpu.make_async_copy(fine_in, fine_out, sems.at[1]),
    ]
    for copy in copies:
        copy.start()
    for copy in copies:
        copy.wait()


def per_device(multipoles, box_scale, fine_list, wedge_index, list_count, fine_ops, phases, coarse_list, coarse_ops):
    n_dir, n_space = lax.axis_size("dir"), lax.axis_size("space")
    boxes, coeffs = multipoles.shape
    group = n_dir * boxes
    half = n_dir // 2
    inside = half * boxes
    dirs, _, terms = coarse_list.shape
    wedges = fine_ops.shape[0]
    list_width = fine_list.shape[1]
    block_boxes = 16
    blocks = boxes // block_boxes
    lists = jnp.transpose(coarse_list, (0, 2, 1))

    hbm = pl.BlockSpec(memory_space=pltpu.HBM)
    members = blocks * block_boxes * wedges
    limit = (20 << 20) + 4 * dirs * group * (inside + 2 * coeffs) + 2 * members * group
    outs = pl.pallas_call(
        functools.partial(kernel, n_dir, n_space, boxes, dirs, block_boxes),
        out_shape=(
            jax.ShapeDtypeStruct((boxes, coeffs), F32),
            jax.ShapeDtypeStruct((n_dir * dirs, boxes, coeffs), BF16),
        ),
        in_specs=[hbm] * 9,
        out_specs=(pl.BlockSpec(memory_space=pl.ANY), pl.BlockSpec(memory_space=pl.ANY)),
        scratch_shapes=[
            pltpu.VMEM((group + 2 * boxes, coeffs), BF16),
            pltpu.VMEM((n_dir, 1, boxes), F32),
            pltpu.VMEM((dirs, terms, inside), jnp.int32),
            pltpu.VMEM((dirs, terms, inside), jnp.int32),
            pltpu.VMEM((list_width, boxes), jnp.int32),
            pltpu.VMEM((list_width, boxes), jnp.int32),
            pltpu.VMEM((1, boxes), jnp.int32),
            pltpu.VMEM((2, list_width, LANES), jnp.int32),
            pltpu.VMEM(phases.shape, F32),
            pltpu.VMEM(fine_ops.shape, BF16),
            pltpu.VMEM(coarse_ops.shape, BF16),
            pltpu.VMEM((dirs // 2,) + coarse_ops.shape[1:], BF16),
            pltpu.VMEM((inside, dirs * terms), F32),
            pltpu.VMEM((2 * dirs, inside, group), BF16),
            pltpu.VMEM((members, group + 2 * boxes), BF16),
            pltpu.VMEM((2 * dirs, group, coeffs), F32),
            pltpu.VMEM((2 * dirs, group, coeffs), BF16),
            pltpu.VMEM((wedges, boxes, coeffs), BF16),
            pltpu.VMEM((2 * dirs * half, boxes, coeffs), BF16),
            pltpu.VMEM((dirs // 2, inside, coeffs), BF16),
            pltpu.VMEM((dirs // 2, inside, coeffs), BF16),
            pltpu.VMEM((boxes, coeffs), F32),
            pltpu.SemaphoreType.DMA((9,)),
        ] + [pltpu.SemaphoreType.DMA((n,)) for n in (1, 3, 1, 3, 1, 2, 5, 2, 3)],
        compiler_params=pltpu.CompilerParams(
            collective_id=0, has_side_effects=True, vmem_limit_bytes=limit),
        name="translations",
    )(*[
        pltpu.with_memory_space_constraint(value, pltpu.HBM)
        for value in (
            multipoles, box_scale.reshape(1, boxes), lists, fine_list.T, wedge_index.T, list_count.reshape(1, boxes),
            phases, fine_ops, coarse_ops)
    ])
    return pl.pallas_call(
        settle,
        out_shape=tuple(jax.ShapeDtypeStruct(out.shape, out.dtype) for out in outs),
        in_specs=[pl.BlockSpec(memory_space=pltpu.VMEM)] * 2,
        out_specs=tuple(pl.BlockSpec(memory_space=pltpu.HBM) for _ in outs),
        scratch_shapes=[pltpu.SemaphoreType.DMA((2,))],
        name="settle",
    )(*[pltpu.with_memory_space_constraint(out, pltpu.VMEM) for out in outs])


def solution(mesh):
    return jax.shard_map(
        per_device,
        mesh=mesh,
        in_specs=(
            P(("space", "dir"), None),
            P(("space", "dir")),
            P(("space", "dir"), None),
            P(("space", "dir"), None),
            P(("space", "dir")),
            P(),
            P(),
            P("dir", "space", None),
            P("dir", None, None),
        ),
        out_specs=(P(("space", "dir"), None), P(None, ("space", "dir"), None)),
        check_vma=False,
    )
```

```python
import functools
import math

import jax
import jax.numpy as jnp
from jax import lax
from jax.experimental import pallas as pl
from jax.experimental.pallas import tpu as pltpu
from jax.sharding import PartitionSpec as P

MESH = pl.DeviceIdType.MESH
F32 = jnp.float32
BF16 = jnp.bfloat16
LANES = 128
HALF_TURN_HI = 3.140625
HALF_TURN_LO = 9.67653589793e-4
SINE = (1.0, -0.1666666716337204, 0.008333330973982811, -0.00019840856839437038,
        2.752503405645257e-06, -2.388494557692411e-08)
COSINE = (1.0, -0.5, 0.0416666679084301, -0.0013888884568586946, 2.4801034669508226e-05,
          -2.7524427537174332e-07, 1.9903911852026113e-09)


def horner(terms, x):
    total = jnp.full_like(x, terms[-1])
    for term in terms[-2::-1]:
        total = total * x + term
    return total


def signed_turn(angle):
    turns = jnp.floor(angle * (1.0 / math.pi) + 0.5)
    rest = (angle - turns * HALF_TURN_HI) - turns * HALF_TURN_LO
    halves = turns * 0.5
    sign = 1.0 - 4.0 * (halves - jnp.floor(halves))
    square = rest * rest
    return sign, horner(COSINE, square), horner(SINE, square) * rest


def partner(me, k):
    bit, other = 1, me
    while bit <= k:
        if k & bit:
            other = other + bit * (1 - 2 * ((me // bit) % 2))
        bit *= 2
    return other


def kernel(n_dir, n_space, boxes, dirs, block_boxes, mult, scale, lists, fine_list, wedge_index, list_count, phases,
           fine_ops, coarse_ops,
           fine_out, coarse_out,
           cand, scales, lists_v, far_lists, fine_v, wedge_v, count_v, slots_v, phases_v, fine_ops_v, coarse_ops_v, far_ops,
           columns, counts, weights, turns, rotated, sums, translated, gathered_out, gathered_in, fine_v_out,
           local_sem, rows_send, rows_recv, scale_send, scale_recv, halo_recv, list_sems, ops_sems,
           back_sems):
    me = lax.axis_index("dir")
    space = lax.axis_index("space")
    group = n_dir * boxes
    half = n_dir // 2
    inside = half * boxes
    width = mult.shape[1] // 2
    terms = lists.shape[1]
    wedges = fine_ops.shape[0]
    own = pl.ds(pl.multiple_of(me * boxes, boxes), boxes)
    above = lax.rem(space + 1, n_space)
    below = lax.rem(space + n_space - 1, n_space)
    core = lax.rem(space, 2)
    sibling = space + 1 - 2 * core
    far = partner(me, half)
    base = me // half * half
    first_inside = pl.multiple_of(base * boxes, inside)
    first_far = pl.multiple_of((half - base) * boxes, inside)
    share_dirs = dirs // 2
    level = space // 2
    levels = n_space // 2
    shared_deep = coarse_ops.shape[1] // 2
    deep = shared_deep // levels
    passed = pl.ds(pl.multiple_of(level * deep, deep), deep)
    common = pl.ds(shared_deep, coarse_ops.shape[1] - shared_deep)
    storeys = [2 * lax.rem(level + i, levels) + core for i in range(1, levels)]
    share = pl.ds(core * share_dirs, share_dirs)

    barrier = pltpu.get_barrier_semaphore()
    for k in range(1, half + 1):
        pl.semaphore_signal(barrier, inc=1, device_id={"dir": partner(me, k)}, device_id_type=MESH)
    for k in range(1, half):
        pl.semaphore_signal(
            barrier, inc=1, device_id={"dir": partner(me, k), "space": sibling}, device_id_type=MESH)
    for other in [above, below] + storeys:
        pl.semaphore_signal(barrier, inc=1, device_id={"space": other}, device_id_type=MESH)

    pulls = [
        pltpu.make_async_copy(lists.at[:, :, pl.ds(first_inside, inside)], lists_v, local_sem.at[0]),
        pltpu.make_async_copy(fine_list, fine_v, local_sem.at[1]),
        pltpu.make_async_copy(wedge_index, wedge_v, local_sem.at[2]),
        pltpu.make_async_copy(mult, cand.at[own], local_sem.at[3]),
        pltpu.make_async_copy(scale, scales.at[me], local_sem.at[4]),
        pltpu.make_async_copy(phases, phases_v, local_sem.at[5]),
        pltpu.make_async_copy(coarse_ops, coarse_ops_v, local_sem.at[6]),
        pltpu.make_async_copy(fine_ops, fine_ops_v, local_sem.at[7]),
        pltpu.make_async_copy(list_count, count_v, local_sem.at[8]),
    ]
    for at in (3, 4, 0, 6, 1, 2, 8, 5, 7):
        pulls[at].start()

    def set_columns(values):
        columns[...] = jnp.transpose(
            jnp.concatenate([values[d].astype(F32) for d in range(dirs)], axis=0))

    def set_counts(first_slot):
        def count_rows(i, carry):
            rows = pl.ds(pl.multiple_of(i * boxes, boxes), boxes)
            ids = columns[rows, :]
            lane = lax.broadcasted_iota(jnp.int32, (boxes, group), 1).astype(F32)
            for d in range(dirs):
                total = jnp.zeros((boxes, group), F32)
                for k in range(terms):
                    at = d * terms + k
                    total = total + jnp.where(ids[:, at:at + 1] == lane, 1.0, 0.0)
                counts[first_slot + d, rows, :] = total.astype(BF16)
            return carry

        lax.fori_loop(0, half, count_rows, 0)

    pl.semaphore_wait(barrier, 2 * half + levels)

    def rows_of(source):
        return pl.ds(pl.multiple_of(source * boxes, boxes), boxes)

    def stage(k):
        return 0 if k < half else 1 if k == half else 2

    def rows_wait(blocks, sem):
        data = cand.at[pl.ds(0, blocks * boxes)]
        pltpu.make_async_copy(data, data, sem).wait()

    def scales_wait(blocks, sem):
        data = scales.at[pl.ds(0, blocks)]
        pltpu.make_async_copy(data, data, sem).wait()

    def send_rows(k, to, data, source):
        pltpu.make_async_remote_copy(
            data, cand.at[rows_of(source)], rows_send.at[0], rows_recv.at[stage(k)],
            device_id={"dir": partner(me, to)}, device_id_type=MESH).start()

    def send_scale(k, to, data, source):
        pltpu.make_async_remote_copy(
            data, scales.at[source], scale_send.at[0], scale_recv.at[stage(k)],
            device_id={"dir": partner(me, to)}, device_id_type=MESH).start()

    pulls[3].wait()
    pulls[4].wait()
    for k in range(half, 0, -1):
        send_scale(k, k, scales.at[me], me)
        send_rows(k, k, cand.at[own], me)
    for side, other in ((0, above), (1, below)):
        pltpu.make_async_remote_copy(
            mult, cand.at[pl.ds(group + side * boxes, boxes)], rows_send.at[0], halo_recv.at[0],
            device_id={"space": other}, device_id_type=MESH).start()
    list_copy = pltpu.make_async_remote_copy(
        lists.at[:, :, pl.ds(first_far, inside)], far_lists, list_sems.at[0], list_sems.at[1],
        device_id={"dir": far}, device_id_type=MESH)
    list_copy.start()
    ops_copies = [pltpu.make_async_remote_copy(
        coarse_ops_v.at[share, rows], far_ops.at[:, rows],
        rows_send.at[0], ops_sems.at[1 + at], device_id={"dir": far}, device_id_type=MESH)
        for at, rows in enumerate((passed, common))]

    pulls[0].wait()
    set_columns(lists_v)
    set_counts(0)
    pulls[6].wait()

    pulls[1].wait()
    pulls[2].wait()
    pulls[8].wait()
    blocks = boxes // block_boxes
    members = block_boxes * wedges
    width_list = fine_v.shape[0]
    first = fine_v[...] - space * group
    slot_values = jnp.where(
        first < 0, first + (2 * group - me * boxes), jnp.where(first < group, first, first + (boxes - me * boxes)))
    box = lax.broadcasted_iota(jnp.int32, (width_list, boxes), 1)
    term = lax.broadcasted_iota(jnp.int32, (width_list, boxes), 0)
    code_values = jnp.where(term < count_v[...], wedge_v[...] * block_boxes + box % block_boxes, -1)
    packs = LANES // block_boxes
    depth = width_list // packs
    blank = jnp.zeros((width_list, LANES - boxes), jnp.int32)
    slots_v[0] = jnp.concatenate([slot_values, blank], axis=1)
    slots_v[1] = jnp.concatenate([code_values, blank], axis=1)
    pack = lax.broadcasted_iota(jnp.int32, (depth, LANES), 1) // block_boxes

    def cells_of(which, g):
        row = jnp.zeros((depth, LANES), jnp.int32)
        for p in range(packs):
            row = jnp.where(pack == (g + p) % packs, turned[which][p], row)
        if g:
            row = pltpu.roll(row, LANES - g * block_boxes, 1)
        return jnp.concatenate([row[t:t + 1, :] for t in range(depth)], axis=1)

    turned = []
    for which in range(2):
        pieces = [slots_v[which, p * depth:(p + 1) * depth, :] for p in range(packs)]
        turned.append([pieces[0]] + [pltpu.roll(pieces[p], p * block_boxes, 1) for p in range(1, packs)])
    cells = depth * LANES
    for g in range(blocks):
        member = lax.broadcasted_iota(jnp.int32, (members, cells), 0)
        mask = jnp.where(member == cells_of(1, g), 1.0, 0.0).astype(BF16)
        candidate = lax.broadcasted_iota(jnp.int32, (cand.shape[0], cells), 0)
        onehot = jnp.where(candidate == cells_of(0, g), 1.0, 0.0).astype(BF16)
        weights[g * members:(g + 1) * members, :] = lax.dot_general(
            mask, onehot, (((1,), (1,)), ((), ())), preferred_element_type=F32).astype(BF16)
        if g == 1:
            for copy in ops_copies:
                copy.start()

    def angles(source):
        column = jnp.transpose(jnp.broadcast_to(scales[source], (8, boxes)))[:, 0:1]
        for slot in range(2 * dirs):
            owner = me if slot < dirs else far
            angle = phases_v[pl.ds(owner * dirs + slot % dirs, 1), :] * column
            sign, cosine, sine = signed_turn(angle)
            turns[slot, rows_of(source), :width] = cosine * sign
            turns[slot, rows_of(source), width:] = sine * sign

    def rotate(source):
        rows = rows_of(source)
        picked = cand[rows, :].astype(F32)
        real, imag = picked[:, :width], picked[:, width:]
        for slot in range(2 * dirs):
            cosine, sine = turns[slot, rows, :width], turns[slot, rows, width:]
            rotated[slot, rows, :width] = (real * cosine - imag * sine).astype(BF16)
            rotated[slot, rows, width:] = (real * sine + imag * cosine).astype(BF16)

    pulls[5].wait()
    angles(me)
    rotate(me)
    scales_wait(1, scale_recv.at[1])
    for k in range(half - 1, 0, -1):
        send_scale(half + k, k, scales.at[far], far)
    rows_wait(1, rows_recv.at[1])
    for k in range(half - 1, 0, -1):
        send_rows(half + k, k, cand.at[rows_of(far)], far)
    angles(far)
    scales_wait(half - 1, scale_recv.at[0])
    for k in range(1, half):
        angles(partner(me, k))
    rotate(far)
    rows_wait(half - 1, rows_recv.at[0])
    for k in range(1, half):
        rotate(partner(me, k))
    list_copy.wait_recv()
    set_columns(far_lists)
    set_counts(dirs)
    scales_wait(half - 1, scale_recv.at[2])
    for k in range(half + 1, n_dir):
        angles(partner(me, k))
    ops_copies[0].wait_recv()
    for other in storeys:
        pltpu.make_async_remote_copy(
            far_ops.at[:, passed], far_ops.at[:, passed], rows_send.at[0], ops_sems.at[0],
            device_id={"space": other}, device_id_type=MESH).start()
    rows_wait(half - 1, rows_recv.at[2])
    for k in range(half + 1, n_dir):
        rotate(partner(me, k))

    def gather(at):
        return jnp.dot(counts[at], rotated[at], preferred_element_type=F32).astype(BF16)

    def translate(gathered, matrix, slot, here, home):
        result = jnp.dot(gathered, matrix, preferred_element_type=F32).astype(BF16)
        first = slot * half
        for member in range(half):
            translated[first + member] = result[member * boxes:(member + 1) * boxes]
        for k in range(half - 1, -1, -1):
            to = partner(me, k)
            piece = translated.at[first + to - base]
            if k or not home:
                where = {"dir": to} if home else {"dir": to, "space": sibling}
                pltpu.make_async_remote_copy(
                    piece, here, rows_send.at[0], back_sems.at[0], device_id=where, device_id_type=MESH).start()
            else:
                pltpu.make_async_copy(piece, here, back_sems.at[1]).start()

    def far_out(i):
        return coarse_out.at[far * dirs + core * share_dirs + i]

    for d in range(dirs):
        translate(gather(d), coarse_ops_v[d], d, coarse_out.at[me * dirs + d], True)
    for i in range(share_dirs):
        gathered_out[i] = gather(dirs + (1 - core) * share_dirs + i)
    swap = pltpu.make_async_remote_copy(
        gathered_out, gathered_in, rows_send.at[0], ops_sems.at[3],
        device_id={"space": sibling}, device_id_type=MESH)
    swap.start()
    own_gathered = [gather(dirs + core * share_dirs + i) for i in range(share_dirs)]
    rest = far_ops.at[:, pl.ds(0, (levels - 1) * deep)]
    pltpu.make_async_copy(rest, rest, ops_sems.at[0]).wait()
    ops_copies[1].wait_recv()
    for i in range(share_dirs):
        translate(own_gathered[i], far_ops[i], dirs + i, far_out(i), True)
    swap.wait_recv()
    for i in range(share_dirs):
        translate(gathered_in[i], far_ops[i], dirs + share_dirs + i, far_out(i), False)

    rows_wait(2, halo_recv.at[0])
    for g in range(blocks):
        total = jnp.dot(weights[g * members:(g + 1) * members, :], cand[...], preferred_element_type=F32).astype(BF16)
        for w in range(wedges):
            sums[w, g * block_boxes:(g + 1) * block_boxes, :] = total[w * block_boxes:(w + 1) * block_boxes]
    pulls[7].wait()
    local = jnp.zeros(fine_v_out.shape, F32)
    for w in range(wedges):
        local = local + jnp.dot(sums[w], fine_ops_v[w], preferred_element_type=F32)
    fine_v_out[...] = local
    fine_copy = pltpu.make_async_copy(fine_v_out, fine_out, local_sem.at[0])
    fine_copy.start()

    fine_copy.wait()
    kept = translated.at[pl.ds(0, dirs + share_dirs)]
    pltpu.make_async_copy(kept, kept, back_sems.at[1]).wait()
    returned = 2 * dirs * half - dirs - share_dirs
    moved = translated.at[pl.ds(0, returned)]
    pltpu.make_async_copy(moved, moved, back_sems.at[0]).wait()
    sent_rows = (
        (n_dir + 1 + returned) * boxes
        + share_dirs * (inside + levels * deep + coarse_ops.shape[1] - shared_deep))
    sent = rotated.at[:, pl.ds(0, sent_rows // (2 * dirs))]
    pltpu.make_async_copy(sent, sent, rows_send.at[0]).wait()
    scales_wait(n_dir - 1, scale_send.at[0])
    list_copy.wait_send()


def settle(fine_in, coarse_in, fine_out, coarse_out, sems):
    copies = [
        pltpu.make_async_copy(coarse_in, coarse_out, sems.at[0]),
        pltpu.make_async_copy(fine_in, fine_out, sems.at[1]),
    ]
    for copy in copies:
        copy.start()
    for copy in copies:
        copy.wait()


def per_device(multipoles, box_scale, fine_list, wedge_index, list_count, fine_ops, phases, coarse_list, coarse_ops):
    n_dir, n_space = lax.axis_size("dir"), lax.axis_size("space")
    boxes, coeffs = multipoles.shape
    group = n_dir * boxes
    half = n_dir // 2
    inside = half * boxes
    dirs, _, terms = coarse_list.shape
    wedges = fine_ops.shape[0]
    list_width = fine_list.shape[1]
    block_boxes = 16
    blocks = boxes // block_boxes
    lists = jnp.transpose(coarse_list, (0, 2, 1))

    hbm = pl.BlockSpec(memory_space=pltpu.HBM)
    members = blocks * block_boxes * wedges
    limit = (20 << 20) + 4 * dirs * group * (inside + 2 * coeffs) + 2 * members * group
    outs = pl.pallas_call(
        functools.partial(kernel, n_dir, n_space, boxes, dirs, block_boxes),
        out_shape=(
            jax.ShapeDtypeStruct((boxes, coeffs), F32),
            jax.ShapeDtypeStruct((n_dir * dirs, boxes, coeffs), BF16),
        ),
        in_specs=[hbm] * 9,
        out_specs=(pl.BlockSpec(memory_space=pl.ANY), pl.BlockSpec(memory_space=pl.ANY)),
        scratch_shapes=[
            pltpu.VMEM((group + 2 * boxes, coeffs), BF16),
            pltpu.VMEM((n_dir, 1, boxes), F32),
            pltpu.VMEM((dirs, terms, inside), jnp.int32),
            pltpu.VMEM((dirs, terms, inside), jnp.int32),
            pltpu.VMEM((list_width, boxes), jnp.int32),
            pltpu.VMEM((list_width, boxes), jnp.int32),
            pltpu.VMEM((1, boxes), jnp.int32),
            pltpu.VMEM((2, list_width, LANES), jnp.int32),
            pltpu.VMEM(phases.shape, F32),
            pltpu.VMEM(fine_ops.shape, BF16),
            pltpu.VMEM(coarse_ops.shape, BF16),
            pltpu.VMEM((dirs // 2,) + coarse_ops.shape[1:], BF16),
            pltpu.VMEM((inside, dirs * terms), F32),
            pltpu.VMEM((2 * dirs, inside, group), BF16),
            pltpu.VMEM((members, group + 2 * boxes), BF16),
            pltpu.VMEM((2 * dirs, group, coeffs), F32),
            pltpu.VMEM((2 * dirs, group, coeffs), BF16),
            pltpu.VMEM((wedges, boxes, coeffs), BF16),
            pltpu.VMEM((2 * dirs * half, boxes, coeffs), BF16),
            pltpu.VMEM((dirs // 2, inside, coeffs), BF16),
            pltpu.VMEM((dirs // 2, inside, coeffs), BF16),
            pltpu.VMEM((boxes, coeffs), F32),
            pltpu.SemaphoreType.DMA((9,)),
        ] + [pltpu.SemaphoreType.DMA((n,)) for n in (1, 3, 1, 3, 1, 2, 4, 2)],
        compiler_params=pltpu.CompilerParams(
            collective_id=0, has_side_effects=True, vmem_limit_bytes=limit),
        name="translations",
    )(*[
        pltpu.with_memory_space_constraint(value, pltpu.HBM)
        for value in (
            multipoles, box_scale.reshape(1, boxes), lists, fine_list.T, wedge_index.T, list_count.reshape(1, boxes),
            phases, fine_ops, coarse_ops)
    ])
    return pl.pallas_call(
        settle,
        out_shape=tuple(jax.ShapeDtypeStruct(out.shape, out.dtype) for out in outs),
        in_specs=[pl.BlockSpec(memory_space=pltpu.VMEM)] * 2,
        out_specs=tuple(pl.BlockSpec(memory_space=pltpu.HBM) for _ in outs),
        scratch_shapes=[pltpu.SemaphoreType.DMA((2,))],
        name="settle",
    )(*[pltpu.with_memory_space_constraint(out, pltpu.VMEM) for out in outs])


def solution(mesh):
    return jax.shard_map(
        per_device,
        mesh=mesh,
        in_specs=(
            P(("space", "dir"), None),
            P(("space", "dir")),
            P(("space", "dir"), None),
            P(("space", "dir"), None),
            P(("space", "dir")),
            P(),
            P(),
            P("dir", "space", None),
            P("dir", None, None),
        ),
        out_specs=(P(("space", "dir"), None), P(None, ("space", "dir"), None)),
        check_vma=False,
    )
```

```python
import functools
import math

import jax
import jax.numpy as jnp
from jax import lax
from jax.experimental import pallas as pl
from jax.experimental.pallas import tpu as pltpu
from jax.sharding import PartitionSpec as P

MESH = pl.DeviceIdType.MESH
F32 = jnp.float32
BF16 = jnp.bfloat16
LANES = 128
HALF_TURN_HI = 3.140625
HALF_TURN_LO = 9.67653589793e-4
SINE = (1.0, -0.1666666716337204, 0.008333330973982811, -0.00019840856839437038,
        2.752503405645257e-06, -2.388494557692411e-08)
COSINE = (1.0, -0.5, 0.0416666679084301, -0.0013888884568586946, 2.4801034669508226e-05,
          -2.7524427537174332e-07, 1.9903911852026113e-09)


def horner(terms, x):
    total = jnp.full_like(x, terms[-1])
    for term in terms[-2::-1]:
        total = total * x + term
    return total


def signed_turn(angle):
    turns = jnp.floor(angle * (1.0 / math.pi) + 0.5)
    rest = (angle - turns * HALF_TURN_HI) - turns * HALF_TURN_LO
    halves = turns * 0.5
    sign = 1.0 - 4.0 * (halves - jnp.floor(halves))
    square = rest * rest
    return sign, horner(COSINE, square), horner(SINE, square) * rest


def partner(me, k):
    bit, other = 1, me
    while bit <= k:
        if k & bit:
            other = other + bit * (1 - 2 * ((me // bit) % 2))
        bit *= 2
    return other


def kernel(n_dir, n_space, boxes, dirs, block_boxes, mult, scale, lists, fine_list, wedge_index, list_count, phases,
           fine_ops, coarse_ops,
           fine_out, coarse_out,
           cand, scales, lists_v, far_lists, fine_v, wedge_v, count_v, slots_v, phases_v, fine_ops_v, coarse_ops_v, far_ops,
           columns, counts, weights, turns, rotated, sums, translated, gathered_out, gathered_in, fine_v_out,
           local_sem, rows_send, rows_recv, scale_send, scale_recv, halo_recv, list_sems, ops_sems,
           back_sems):
    me = lax.axis_index("dir")
    space = lax.axis_index("space")
    group = n_dir * boxes
    half = n_dir // 2
    inside = half * boxes
    width = mult.shape[1] // 2
    terms = lists.shape[1]
    wedges = fine_ops.shape[0]
    own = pl.ds(pl.multiple_of(me * boxes, boxes), boxes)
    above = lax.rem(space + 1, n_space)
    below = lax.rem(space + n_space - 1, n_space)
    core = lax.rem(space, 2)
    sibling = space + 1 - 2 * core
    far = partner(me, half)
    base = me // half * half
    first_inside = pl.multiple_of(base * boxes, inside)
    first_far = pl.multiple_of((half - base) * boxes, inside)
    share_dirs = dirs // 2
    level = space // 2
    levels = n_space // 2
    shared_deep = coarse_ops.shape[1] // 2
    deep = shared_deep // levels
    passed = pl.ds(pl.multiple_of(level * deep, deep), deep)
    common = pl.ds(shared_deep, coarse_ops.shape[1] - shared_deep)
    storeys = [2 * lax.rem(level + i, levels) + core for i in range(1, levels)]
    share = pl.ds(core * share_dirs, share_dirs)

    barrier = pltpu.get_barrier_semaphore()
    for k in range(1, half + 1):
        pl.semaphore_signal(barrier, inc=1, device_id={"dir": partner(me, k)}, device_id_type=MESH)
    greeted = [above, below] + (storeys if levels > 2 else [])
    for other in greeted:
        pl.semaphore_signal(barrier, inc=1, device_id={"space": other}, device_id_type=MESH)

    pulls = [
        pltpu.make_async_copy(lists.at[:, :, pl.ds(first_inside, inside)], lists_v, local_sem.at[0]),
        pltpu.make_async_copy(fine_list, fine_v, local_sem.at[1]),
        pltpu.make_async_copy(wedge_index, wedge_v, local_sem.at[2]),
        pltpu.make_async_copy(mult, cand.at[own], local_sem.at[3]),
        pltpu.make_async_copy(scale, scales.at[me], local_sem.at[4]),
        pltpu.make_async_copy(phases, phases_v, local_sem.at[5]),
        pltpu.make_async_copy(coarse_ops, coarse_ops_v, local_sem.at[6]),
        pltpu.make_async_copy(fine_ops, fine_ops_v, local_sem.at[7]),
        pltpu.make_async_copy(list_count, count_v, local_sem.at[8]),
    ]
    for at in (3, 4, 0, 6, 1, 2, 8, 5, 7):
        pulls[at].start()

    def set_columns(values):
        columns[...] = jnp.transpose(
            jnp.concatenate([values[d].astype(F32) for d in range(dirs)], axis=0))

    def set_counts(first_slot):
        def count_rows(i, carry):
            rows = pl.ds(pl.multiple_of(i * boxes, boxes), boxes)
            ids = columns[rows, :]
            lane = lax.broadcasted_iota(jnp.int32, (boxes, group), 1).astype(F32)
            for d in range(dirs):
                total = jnp.zeros((boxes, group), F32)
                for k in range(terms):
                    at = d * terms + k
                    total = total + jnp.where(ids[:, at:at + 1] == lane, 1.0, 0.0)
                counts[first_slot + d, rows, :] = total.astype(BF16)
            return carry

        lax.fori_loop(0, half, count_rows, 0)

    pl.semaphore_wait(barrier, half + len(greeted))

    def rows_of(source):
        return pl.ds(pl.multiple_of(source * boxes, boxes), boxes)

    def stage(k):
        return 0 if k < half else 1 if k == half else 2

    def rows_wait(blocks, sem):
        data = cand.at[pl.ds(0, blocks * boxes)]
        pltpu.make_async_copy(data, data, sem).wait()

    def scales_wait(blocks, sem):
        data = scales.at[pl.ds(0, blocks)]
        pltpu.make_async_copy(data, data, sem).wait()

    def send_rows(k, to, data, source):
        pltpu.make_async_remote_copy(
            data, cand.at[rows_of(source)], rows_send.at[0], rows_recv.at[stage(k)],
            device_id={"dir": partner(me, to)}, device_id_type=MESH).start()

    def send_scale(k, to, data, source):
        pltpu.make_async_remote_copy(
            data, scales.at[source], scale_send.at[0], scale_recv.at[stage(k)],
            device_id={"dir": partner(me, to)}, device_id_type=MESH).start()

    pulls[3].wait()
    pulls[4].wait()
    for k in range(half, 0, -1):
        send_scale(k, k, scales.at[me], me)
        send_rows(k, k, cand.at[own], me)
    for side, other in ((0, above), (1, below)):
        pltpu.make_async_remote_copy(
            mult, cand.at[pl.ds(group + side * boxes, boxes)], rows_send.at[0], halo_recv.at[0],
            device_id={"space": other}, device_id_type=MESH).start()
    list_copy = pltpu.make_async_remote_copy(
        lists.at[:, :, pl.ds(first_far, inside)], far_lists, list_sems.at[0], list_sems.at[1],
        device_id={"dir": far}, device_id_type=MESH)
    list_copy.start()
    ops_copies = [pltpu.make_async_remote_copy(
        coarse_ops_v.at[share, rows], far_ops.at[:, rows],
        rows_send.at[0], ops_sems.at[1 + at], device_id={"dir": far}, device_id_type=MESH)
        for at, rows in enumerate((passed, common))]

    pulls[0].wait()
    set_columns(lists_v)
    set_counts(0)
    pulls[6].wait()

    pulls[1].wait()
    pulls[2].wait()
    pulls[8].wait()
    blocks = boxes // block_boxes
    members = block_boxes * wedges
    width_list = fine_v.shape[0]
    first = fine_v[...] - space * group
    slot_values = jnp.where(
        first < 0, first + (2 * group - me * boxes), jnp.where(first < group, first, first + (boxes - me * boxes)))
    box = lax.broadcasted_iota(jnp.int32, (width_list, boxes), 1)
    term = lax.broadcasted_iota(jnp.int32, (width_list, boxes), 0)
    code_values = jnp.where(term < count_v[...], wedge_v[...] * block_boxes + box % block_boxes, -1)
    packs = LANES // block_boxes
    depth = width_list // packs
    blank = jnp.zeros((width_list, LANES - boxes), jnp.int32)
    slots_v[0] = jnp.concatenate([slot_values, blank], axis=1)
    slots_v[1] = jnp.concatenate([code_values, blank], axis=1)
    pack = lax.broadcasted_iota(jnp.int32, (depth, LANES), 1) // block_boxes

    def cells_of(which, g):
        row = jnp.zeros((depth, LANES), jnp.int32)
        for p in range(packs):
            row = jnp.where(pack == (g + p) % packs, turned[which][p], row)
        if g:
            row = pltpu.roll(row, LANES - g * block_boxes, 1)
        return jnp.concatenate([row[t:t + 1, :] for t in range(depth)], axis=1)

    turned = []
    for which in range(2):
        pieces = [slots_v[which, p * depth:(p + 1) * depth, :] for p in range(packs)]
        turned.append([pieces[0]] + [pltpu.roll(pieces[p], p * block_boxes, 1) for p in range(1, packs)])
    cells = depth * LANES
    for g in range(blocks):
        member = lax.broadcasted_iota(jnp.int32, (members, cells), 0)
        mask = jnp.where(member == cells_of(1, g), 1.0, 0.0).astype(BF16)
        candidate = lax.broadcasted_iota(jnp.int32, (cand.shape[0], cells), 0)
        onehot = jnp.where(candidate == cells_of(0, g), 1.0, 0.0).astype(BF16)
        weights[g * members:(g + 1) * members, :] = lax.dot_general(
            mask, onehot, (((1,), (1,)), ((), ())), preferred_element_type=F32).astype(BF16)
        if g == 1:
            for copy in ops_copies:
                copy.start()

    def angles(source):
        column = jnp.transpose(jnp.broadcast_to(scales[source], (8, boxes)))[:, 0:1]
        for slot in range(2 * dirs):
            owner = me if slot < dirs else far
            angle = phases_v[pl.ds(owner * dirs + slot % dirs, 1), :] * column
            sign, cosine, sine = signed_turn(angle)
            turns[slot, rows_of(source), :width] = cosine * sign
            turns[slot, rows_of(source), width:] = sine * sign

    def rotate(source):
        rows = rows_of(source)
        picked = cand[rows, :].astype(F32)
        real, imag = picked[:, :width], picked[:, width:]
        for slot in range(2 * dirs):
            cosine, sine = turns[slot, rows, :width], turns[slot, rows, width:]
            rotated[slot, rows, :width] = (real * cosine - imag * sine).astype(BF16)
            rotated[slot, rows, width:] = (real * sine + imag * cosine).astype(BF16)

    pulls[5].wait()
    angles(me)
    rotate(me)
    scales_wait(1, scale_recv.at[1])
    for k in range(half - 1, 0, -1):
        send_scale(half + k, k, scales.at[far], far)
    rows_wait(1, rows_recv.at[1])
    for k in range(half - 1, 0, -1):
        send_rows(half + k, k, cand.at[rows_of(far)], far)
    angles(far)
    scales_wait(half - 1, scale_recv.at[0])
    for k in range(1, half):
        angles(partner(me, k))
    rotate(far)
    rows_wait(half - 1, rows_recv.at[0])
    for k in range(1, half):
        rotate(partner(me, k))
    list_copy.wait_recv()
    set_columns(far_lists)
    set_counts(dirs)
    scales_wait(half - 1, scale_recv.at[2])
    for k in range(half + 1, n_dir):
        angles(partner(me, k))
    rows_wait(2, halo_recv.at[0])
    ops_copies[0].wait_recv()
    for other in storeys:
        pltpu.make_async_remote_copy(
            far_ops.at[:, passed], far_ops.at[:, passed], rows_send.at[0], ops_sems.at[0],
            device_id={"space": other}, device_id_type=MESH).start()
    rows_wait(half - 1, rows_recv.at[2])
    for k in range(half + 1, n_dir):
        rotate(partner(me, k))

    def gather(at):
        return jnp.dot(counts[at], rotated[at], preferred_element_type=F32).astype(BF16)

    def translate(gathered, matrix, slot, here, home):
        result = jnp.dot(gathered, matrix, preferred_element_type=F32).astype(BF16)
        first = slot * half
        for member in range(half):
            translated[first + member] = result[member * boxes:(member + 1) * boxes]
        for k in range(half - 1, -1, -1):
            to = partner(me, k)
            piece = translated.at[first + to - base]
            if k or not home:
                where = {"dir": to} if home else {"dir": to, "space": sibling}
                pltpu.make_async_remote_copy(
                    piece, here, rows_send.at[0], back_sems.at[0], device_id=where, device_id_type=MESH).start()
            else:
                pltpu.make_async_copy(piece, here, back_sems.at[1]).start()

    def far_out(i):
        return coarse_out.at[far * dirs + core * share_dirs + i]

    for d in range(dirs):
        translate(gather(d), coarse_ops_v[d], d, coarse_out.at[me * dirs + d], True)
    for i in range(share_dirs):
        gathered_out[i] = gather(dirs + (1 - core) * share_dirs + i)
    swap = pltpu.make_async_remote_copy(
        gathered_out, gathered_in, rows_send.at[0], ops_sems.at[3],
        device_id={"space": sibling}, device_id_type=MESH)
    swap.start()
    own_gathered = [gather(dirs + core * share_dirs + i) for i in range(share_dirs)]
    rest = far_ops.at[:, pl.ds(0, (levels - 1) * deep)]
    pltpu.make_async_copy(rest, rest, ops_sems.at[0]).wait()
    ops_copies[1].wait_recv()
    for i in range(share_dirs):
        translate(own_gathered[i], far_ops[i], dirs + i, far_out(i), True)
    swap.wait_recv()
    for i in range(share_dirs):
        translate(gathered_in[i], far_ops[i], dirs + share_dirs + i, far_out(i), False)

    for g in range(blocks):
        total = jnp.dot(weights[g * members:(g + 1) * members, :], cand[...], preferred_element_type=F32).astype(BF16)
        for w in range(wedges):
            sums[w, g * block_boxes:(g + 1) * block_boxes, :] = total[w * block_boxes:(w + 1) * block_boxes]
    pulls[7].wait()
    local = jnp.zeros(fine_v_out.shape, F32)
    for w in range(wedges):
        local = local + jnp.dot(sums[w], fine_ops_v[w], preferred_element_type=F32)
    fine_v_out[...] = local
    fine_copy = pltpu.make_async_copy(fine_v_out, fine_out, local_sem.at[0])
    fine_copy.start()

    fine_copy.wait()
    kept = translated.at[pl.ds(0, dirs + share_dirs)]
    pltpu.make_async_copy(kept, kept, back_sems.at[1]).wait()
    returned = 2 * dirs * half - dirs - share_dirs
    moved = translated.at[pl.ds(0, returned)]
    pltpu.make_async_copy(moved, moved, back_sems.at[0]).wait()
    sent_rows = (
        (n_dir + 1 + returned) * boxes
        + share_dirs * (inside + levels * deep + coarse_ops.shape[1] - shared_deep))
    sent = rotated.at[:, pl.ds(0, sent_rows // (2 * dirs))]
    pltpu.make_async_copy(sent, sent, rows_send.at[0]).wait()
    scales_wait(n_dir - 1, scale_send.at[0])
    list_copy.wait_send()


def settle(fine_in, coarse_in, fine_out, coarse_out, sems):
    copies = [
        pltpu.make_async_copy(coarse_in, coarse_out, sems.at[0]),
        pltpu.make_async_copy(fine_in, fine_out, sems.at[1]),
    ]
    for copy in copies:
        copy.start()
    for copy in copies:
        copy.wait()


def per_device(multipoles, box_scale, fine_list, wedge_index, list_count, fine_ops, phases, coarse_list, coarse_ops):
    n_dir, n_space = lax.axis_size("dir"), lax.axis_size("space")
    boxes, coeffs = multipoles.shape
    group = n_dir * boxes
    half = n_dir // 2
    inside = half * boxes
    dirs, _, terms = coarse_list.shape
    wedges = fine_ops.shape[0]
    list_width = fine_list.shape[1]
    block_boxes = 16
    blocks = boxes // block_boxes
    lists = jnp.transpose(coarse_list, (0, 2, 1))

    hbm = pl.BlockSpec(memory_space=pltpu.HBM)
    members = blocks * block_boxes * wedges
    limit = (20 << 20) + 4 * dirs * group * (inside + 2 * coeffs) + 2 * members * group
    outs = pl.pallas_call(
        functools.partial(kernel, n_dir, n_space, boxes, dirs, block_boxes),
        out_shape=(
            jax.ShapeDtypeStruct((boxes, coeffs), F32),
            jax.ShapeDtypeStruct((n_dir * dirs, boxes, coeffs), BF16),
        ),
        in_specs=[hbm] * 9,
        out_specs=(pl.BlockSpec(memory_space=pl.ANY), pl.BlockSpec(memory_space=pl.ANY)),
        scratch_shapes=[
            pltpu.VMEM((group + 2 * boxes, coeffs), BF16),
            pltpu.VMEM((n_dir, 1, boxes), F32),
            pltpu.VMEM((dirs, terms, inside), jnp.int32),
            pltpu.VMEM((dirs, terms, inside), jnp.int32),
            pltpu.VMEM((list_width, boxes), jnp.int32),
            pltpu.VMEM((list_width, boxes), jnp.int32),
            pltpu.VMEM((1, boxes), jnp.int32),
            pltpu.VMEM((2, list_width, LANES), jnp.int32),
            pltpu.VMEM(phases.shape, F32),
            pltpu.VMEM(fine_ops.shape, BF16),
            pltpu.VMEM(coarse_ops.shape, BF16),
            pltpu.VMEM((dirs // 2,) + coarse_ops.shape[1:], BF16),
            pltpu.VMEM((inside, dirs * terms), F32),
            pltpu.VMEM((2 * dirs, inside, group), BF16),
            pltpu.VMEM((members, group + 2 * boxes), BF16),
            pltpu.VMEM((2 * dirs, group, coeffs), F32),
            pltpu.VMEM((2 * dirs, group, coeffs), BF16),
            pltpu.VMEM((wedges, boxes, coeffs), BF16),
            pltpu.VMEM((2 * dirs * half, boxes, coeffs), BF16),
            pltpu.VMEM((dirs // 2, inside, coeffs), BF16),
            pltpu.VMEM((dirs // 2, inside, coeffs), BF16),
            pltpu.VMEM((boxes, coeffs), F32),
            pltpu.SemaphoreType.DMA((9,)),
        ] + [pltpu.SemaphoreType.DMA((n,)) for n in (1, 3, 1, 3, 1, 2, 4, 2)],
        compiler_params=pltpu.CompilerParams(
            collective_id=0, has_side_effects=True, vmem_limit_bytes=limit),
        name="translations",
    )(*[
        pltpu.with_memory_space_constraint(value, pltpu.HBM)
        for value in (
            multipoles, box_scale.reshape(1, boxes), lists, fine_list.T, wedge_index.T, list_count.reshape(1, boxes),
            phases, fine_ops, coarse_ops)
    ])
    return pl.pallas_call(
        settle,
        out_shape=tuple(jax.ShapeDtypeStruct(out.shape, out.dtype) for out in outs),
        in_specs=[pl.BlockSpec(memory_space=pltpu.VMEM)] * 2,
        out_specs=tuple(pl.BlockSpec(memory_space=pltpu.HBM) for _ in outs),
        scratch_shapes=[pltpu.SemaphoreType.DMA((2,))],
        name="settle",
    )(*[pltpu.with_memory_space_constraint(out, pltpu.VMEM) for out in outs])


def solution(mesh):
    return jax.shard_map(
        per_device,
        mesh=mesh,
        in_specs=(
            P(("space", "dir"), None),
            P(("space", "dir")),
            P(("space", "dir"), None),
            P(("space", "dir"), None),
            P(("space", "dir")),
            P(),
            P(),
            P("dir", "space", None),
            P("dir", None, None),
        ),
        out_specs=(P(("space", "dir"), None), P(None, ("space", "dir"), None)),
        check_vma=False,
    )
```

```python
import functools
import math

import jax
import jax.numpy as jnp
from jax import lax
from jax.experimental import pallas as pl
from jax.experimental.pallas import tpu as pltpu
from jax.sharding import PartitionSpec as P

MESH = pl.DeviceIdType.MESH
F32 = jnp.float32
BF16 = jnp.bfloat16
LANES = 128
HALF_TURN_HI = 3.140625
HALF_TURN_LO = 9.67653589793e-4
SINE = (1.0, -0.1666666716337204, 0.008333330973982811, -0.00019840856839437038,
        2.752503405645257e-06, -2.388494557692411e-08)
COSINE = (1.0, -0.5, 0.0416666679084301, -0.0013888884568586946, 2.4801034669508226e-05,
          -2.7524427537174332e-07, 1.9903911852026113e-09)


def horner(terms, x):
    total = jnp.full_like(x, terms[-1])
    for term in terms[-2::-1]:
        total = total * x + term
    return total


def signed_turn(angle):
    turns = jnp.floor(angle * (1.0 / math.pi) + 0.5)
    rest = (angle - turns * HALF_TURN_HI) - turns * HALF_TURN_LO
    halves = turns * 0.5
    sign = 1.0 - 4.0 * (halves - jnp.floor(halves))
    square = rest * rest
    return sign, horner(COSINE, square), horner(SINE, square) * rest


def partner(me, k):
    bit, other = 1, me
    while bit <= k:
        if k & bit:
            other = other + bit * (1 - 2 * ((me // bit) % 2))
        bit *= 2
    return other


def kernel(n_dir, n_space, boxes, dirs, block_boxes, mult, scale, lists, fine_list, wedge_index, list_count, phases,
           fine_ops, coarse_ops,
           fine_out, coarse_out,
           cand, scales, lists_v, far_lists, pairs_v, count_v, slots_v, phases_v, fine_ops_v, coarse_ops_v, far_ops,
           columns, counts, weights, turns, rotated, sums, translated, gathered_out, gathered_in, fine_v_out,
           local_sem, rows_send, rows_recv, scale_send, scale_recv, halo_recv, list_sems, ops_sems,
           back_sems):
    me = lax.axis_index("dir")
    space = lax.axis_index("space")
    group = n_dir * boxes
    half = n_dir // 2
    inside = half * boxes
    width = mult.shape[1] // 2
    terms = lists.shape[1]
    wedges = fine_ops.shape[0]
    own = pl.ds(pl.multiple_of(me * boxes, boxes), boxes)
    above = lax.rem(space + 1, n_space)
    below = lax.rem(space + n_space - 1, n_space)
    core = lax.rem(space, 2)
    sibling = space + 1 - 2 * core
    far = partner(me, half)
    base = me // half * half
    first_inside = pl.multiple_of(base * boxes, inside)
    first_far = pl.multiple_of((half - base) * boxes, inside)
    share_dirs = dirs // 2
    level = space // 2
    levels = n_space // 2
    shared_deep = coarse_ops.shape[1] // 2
    deep = shared_deep // levels
    passed = pl.ds(pl.multiple_of(level * deep, deep), deep)
    common = pl.ds(shared_deep, coarse_ops.shape[1] - shared_deep)
    storeys = [2 * lax.rem(level + i, levels) + core for i in range(1, levels)]
    share = pl.ds(core * share_dirs, share_dirs)

    barrier = pltpu.get_barrier_semaphore()
    for k in range(1, half + 1):
        pl.semaphore_signal(barrier, inc=1, device_id={"dir": partner(me, k)}, device_id_type=MESH)
    greeted = [above, below] + (storeys if levels > 2 else [])
    for other in greeted:
        pl.semaphore_signal(barrier, inc=1, device_id={"space": other}, device_id_type=MESH)

    pulls = [
        pltpu.make_async_copy(lists.at[:, :, pl.ds(first_inside, inside)], lists_v, local_sem.at[0]),
        pltpu.make_async_copy(fine_list, pairs_v.at[0], local_sem.at[1]),
        pltpu.make_async_copy(wedge_index, pairs_v.at[1], local_sem.at[1]),
        pltpu.make_async_copy(mult, cand.at[own], local_sem.at[3]),
        pltpu.make_async_copy(scale, scales.at[me], local_sem.at[4]),
        pltpu.make_async_copy(phases, phases_v, local_sem.at[5]),
        pltpu.make_async_copy(coarse_ops, coarse_ops_v, local_sem.at[6]),
        pltpu.make_async_copy(fine_ops, fine_ops_v, local_sem.at[7]),
        pltpu.make_async_copy(list_count, count_v, local_sem.at[2]),
    ]
    for at in (3, 4, 0, 6, 1, 2, 8, 5, 7):
        pulls[at].start()

    def set_columns(values):
        columns[...] = jnp.transpose(
            jnp.concatenate([values[d].astype(F32) for d in range(dirs)], axis=0))

    def set_counts(first_slot):
        def count_rows(i, carry):
            rows = pl.ds(pl.multiple_of(i * boxes, boxes), boxes)
            ids = columns[rows, :]
            lane = lax.broadcasted_iota(jnp.int32, (boxes, group), 1).astype(F32)
            for d in range(dirs):
                total = jnp.zeros((boxes, group), F32)
                for k in range(terms):
                    at = d * terms + k
                    total = total + jnp.where(ids[:, at:at + 1] == lane, 1.0, 0.0)
                counts[first_slot + d, rows, :] = total.astype(BF16)
            return carry

        lax.fori_loop(0, half, count_rows, 0)

    pl.semaphore_wait(barrier, half + len(greeted))

    def rows_of(source):
        return pl.ds(pl.multiple_of(source * boxes, boxes), boxes)

    def stage(k):
        return 0 if k < half else 1 if k == half else 2

    def rows_wait(blocks, sem):
        data = cand.at[pl.ds(0, blocks * boxes)]
        pltpu.make_async_copy(data, data, sem).wait()

    def scales_wait(blocks, sem):
        data = scales.at[pl.ds(0, blocks)]
        pltpu.make_async_copy(data, data, sem).wait()

    def send_rows(k, to, data, source):
        pltpu.make_async_remote_copy(
            data, cand.at[rows_of(source)], rows_send.at[0], rows_recv.at[stage(k)],
            device_id={"dir": partner(me, to)}, device_id_type=MESH).start()

    def send_scale(k, to, data, source):
        pltpu.make_async_remote_copy(
            data, scales.at[source], scale_send.at[0], scale_recv.at[stage(k)],
            device_id={"dir": partner(me, to)}, device_id_type=MESH).start()

    pulls[3].wait()
    pulls[4].wait()
    for k in range(half, 0, -1):
        send_scale(k, k, scales.at[me], me)
        send_rows(k, k, cand.at[own], me)
    for side, other in ((0, above), (1, below)):
        pltpu.make_async_remote_copy(
            cand.at[own], cand.at[pl.ds(group + side * boxes, boxes)], rows_send.at[0], halo_recv.at[0],
            device_id={"space": other}, device_id_type=MESH).start()
    list_copy = pltpu.make_async_remote_copy(
        lists.at[:, :, pl.ds(first_far, inside)], far_lists, list_sems.at[0], list_sems.at[1],
        device_id={"dir": far}, device_id_type=MESH)
    list_copy.start()
    ops_copies = [pltpu.make_async_remote_copy(
        coarse_ops_v.at[share, rows], far_ops.at[:, rows],
        rows_send.at[0], ops_sems.at[1 + at], device_id={"dir": far}, device_id_type=MESH)
        for at, rows in enumerate((passed, common))]

    pulls[0].wait()
    set_columns(lists_v)
    set_counts(0)
    pulls[6].wait()

    pltpu.make_async_copy(pairs_v, pairs_v, local_sem.at[1]).wait()
    pulls[8].wait()
    blocks = boxes // block_boxes
    members = block_boxes * wedges
    width_list = pairs_v.shape[1]
    first = pairs_v[0] - space * group
    slot_values = jnp.where(
        first < 0, first + (2 * group - me * boxes), jnp.where(first < group, first, first + (boxes - me * boxes)))
    box = lax.broadcasted_iota(jnp.int32, (width_list, boxes), 1)
    term = lax.broadcasted_iota(jnp.int32, (width_list, boxes), 0)
    code_values = jnp.where(term < count_v[...], pairs_v[1] * block_boxes + box % block_boxes, -1)
    packs = LANES // block_boxes
    depth = width_list // packs
    blank = jnp.zeros((width_list, LANES - boxes), jnp.int32)
    slots_v[0] = jnp.concatenate([slot_values, blank], axis=1)
    slots_v[1] = jnp.concatenate([code_values, blank], axis=1)
    pack = lax.broadcasted_iota(jnp.int32, (depth, LANES), 1) // block_boxes

    def cells_of(which, g):
        row = jnp.zeros((depth, LANES), jnp.int32)
        for p in range(packs):
            row = jnp.where(pack == (g + p) % packs, turned[which][p], row)
        if g:
            row = pltpu.roll(row, LANES - g * block_boxes, 1)
        return jnp.concatenate([row[t:t + 1, :] for t in range(depth)], axis=1)

    turned = []
    for which in range(2):
        pieces = [slots_v[which, p * depth:(p + 1) * depth, :] for p in range(packs)]
        turned.append([pieces[0]] + [pltpu.roll(pieces[p], p * block_boxes, 1) for p in range(1, packs)])
    cells = depth * LANES
    for g in range(blocks):
        member = lax.broadcasted_iota(jnp.int32, (members, cells), 0)
        mask = jnp.where(member == cells_of(1, g), 1.0, 0.0).astype(BF16)
        candidate = lax.broadcasted_iota(jnp.int32, (cand.shape[0], cells), 0)
        onehot = jnp.where(candidate == cells_of(0, g), 1.0, 0.0).astype(BF16)
        weights[g * members:(g + 1) * members, :] = lax.dot_general(
            mask, onehot, (((1,), (1,)), ((), ())), preferred_element_type=F32).astype(BF16)
        if g == 1:
            for copy in ops_copies:
                copy.start()

    def angles(source):
        column = jnp.transpose(jnp.broadcast_to(scales[source], (8, boxes)))[:, 0:1]
        for slot in range(2 * dirs):
            owner = me if slot < dirs else far
            angle = phases_v[pl.ds(owner * dirs + slot % dirs, 1), :] * column
            sign, cosine, sine = signed_turn(angle)
            turns[slot, rows_of(source), :width] = cosine * sign
            turns[slot, rows_of(source), width:] = sine * sign

    def rotate(source):
        rows = rows_of(source)
        picked = cand[rows, :].astype(F32)
        real, imag = picked[:, :width], picked[:, width:]
        for slot in range(2 * dirs):
            cosine, sine = turns[slot, rows, :width], turns[slot, rows, width:]
            rotated[slot, rows, :width] = (real * cosine - imag * sine).astype(BF16)
            rotated[slot, rows, width:] = (real * sine + imag * cosine).astype(BF16)

    pulls[5].wait()
    angles(me)
    rotate(me)
    scales_wait(1, scale_recv.at[1])
    for k in range(half - 1, 0, -1):
        send_scale(half + k, k, scales.at[far], far)
    rows_wait(1, rows_recv.at[1])
    for k in range(half - 1, 0, -1):
        send_rows(half + k, k, cand.at[rows_of(far)], far)
    angles(far)
    scales_wait(half - 1, scale_recv.at[0])
    for k in range(1, half):
        angles(partner(me, k))
    rotate(far)
    rows_wait(half - 1, rows_recv.at[0])
    for k in range(1, half):
        rotate(partner(me, k))
    list_copy.wait_recv()
    set_columns(far_lists)
    set_counts(dirs)
    scales_wait(half - 1, scale_recv.at[2])
    for k in range(half + 1, n_dir):
        angles(partner(me, k))
    rows_wait(2, halo_recv.at[0])
    ops_copies[0].wait_recv()
    for other in storeys:
        pltpu.make_async_remote_copy(
            far_ops.at[:, passed], far_ops.at[:, passed], rows_send.at[0], ops_sems.at[0],
            device_id={"space": other}, device_id_type=MESH).start()
    rows_wait(half - 1, rows_recv.at[2])
    for k in range(half + 1, n_dir):
        rotate(partner(me, k))

    def gather(at):
        return jnp.dot(counts[at], rotated[at], preferred_element_type=F32).astype(BF16)

    def translate(gathered, matrix, slot, here, home):
        result = jnp.dot(gathered, matrix, preferred_element_type=F32).astype(BF16)
        first = slot * half
        for member in range(half):
            translated[first + member] = result[member * boxes:(member + 1) * boxes]
        for k in range(half - 1, -1, -1):
            to = partner(me, k)
            piece = translated.at[first + to - base]
            if k or not home:
                where = {"dir": to} if home else {"dir": to, "space": sibling}
                pltpu.make_async_remote_copy(
                    piece, here, rows_send.at[0], back_sems.at[0], device_id=where, device_id_type=MESH).start()
            else:
                pltpu.make_async_copy(piece, here, local_sem.at[1]).start()

    def far_out(i):
        return coarse_out.at[far * dirs + core * share_dirs + i]

    for d in range(dirs):
        translate(gather(d), coarse_ops_v[d], d, coarse_out.at[me * dirs + d], True)
    for i in range(share_dirs):
        gathered_out[i] = gather(dirs + (1 - core) * share_dirs + i)
    swap = pltpu.make_async_remote_copy(
        gathered_out, gathered_in, rows_send.at[0], ops_sems.at[3],
        device_id={"space": sibling}, device_id_type=MESH)
    swap.start()
    own_gathered = [gather(dirs + core * share_dirs + i) for i in range(share_dirs)]
    rest = far_ops.at[:, pl.ds(0, (levels - 1) * deep)]
    pltpu.make_async_copy(rest, rest, ops_sems.at[0]).wait()
    ops_copies[1].wait_recv()
    for i in range(share_dirs):
        translate(own_gathered[i], far_ops[i], dirs + i, far_out(i), True)
    swap.wait_recv()
    for i in range(share_dirs):
        translate(gathered_in[i], far_ops[i], dirs + share_dirs + i, far_out(i), False)

    for g in range(blocks):
        total = jnp.dot(weights[g * members:(g + 1) * members, :], cand[...], preferred_element_type=F32).astype(BF16)
        for w in range(wedges):
            sums[w, g * block_boxes:(g + 1) * block_boxes, :] = total[w * block_boxes:(w + 1) * block_boxes]
    pulls[7].wait()
    local = jnp.zeros(fine_v_out.shape, F32)
    for w in range(wedges):
        local = local + jnp.dot(sums[w], fine_ops_v[w], preferred_element_type=F32)
    fine_v_out[...] = local
    fine_copy = pltpu.make_async_copy(fine_v_out, fine_out, local_sem.at[0])
    fine_copy.start()

    fine_copy.wait()
    kept = translated.at[pl.ds(0, dirs + share_dirs)]
    pltpu.make_async_copy(kept, kept, local_sem.at[1]).wait()
    returned = 2 * dirs * half - dirs - share_dirs
    moved = translated.at[pl.ds(0, returned)]
    pltpu.make_async_copy(moved, moved, back_sems.at[0]).wait()
    sent_rows = (
        (n_dir + 1 + returned) * boxes
        + share_dirs * (inside + levels * deep + coarse_ops.shape[1] - shared_deep))
    sent = rotated.at[:, pl.ds(0, sent_rows // (2 * dirs))]
    pltpu.make_async_copy(sent, sent, rows_send.at[0]).wait()
    scales_wait(n_dir - 1, scale_send.at[0])
    list_copy.wait_send()


def settle(fine_in, coarse_in, fine_out, coarse_out, sems):
    copies = [
        pltpu.make_async_copy(coarse_in, coarse_out, sems.at[0]),
        pltpu.make_async_copy(fine_in, fine_out, sems.at[1]),
    ]
    for copy in copies:
        copy.start()
    for copy in copies:
        copy.wait()


def per_device(multipoles, box_scale, fine_list, wedge_index, list_count, fine_ops, phases, coarse_list, coarse_ops):
    n_dir, n_space = lax.axis_size("dir"), lax.axis_size("space")
    boxes, coeffs = multipoles.shape
    group = n_dir * boxes
    half = n_dir // 2
    inside = half * boxes
    dirs, _, terms = coarse_list.shape
    wedges = fine_ops.shape[0]
    list_width = fine_list.shape[1]
    block_boxes = 16
    blocks = boxes // block_boxes
    lists = jnp.transpose(coarse_list, (0, 2, 1))

    hbm = pl.BlockSpec(memory_space=pltpu.HBM)
    members = blocks * block_boxes * wedges
    limit = (20 << 20) + 4 * dirs * group * (inside + 2 * coeffs) + 2 * members * group
    outs = pl.pallas_call(
        functools.partial(kernel, n_dir, n_space, boxes, dirs, block_boxes),
        out_shape=(
            jax.ShapeDtypeStruct((boxes, coeffs), F32),
            jax.ShapeDtypeStruct((n_dir * dirs, boxes, coeffs), BF16),
        ),
        in_specs=[hbm] * 9,
        out_specs=(pl.BlockSpec(memory_space=pl.ANY), pl.BlockSpec(memory_space=pl.ANY)),
        scratch_shapes=[
            pltpu.VMEM((group + 2 * boxes, coeffs), BF16),
            pltpu.VMEM((n_dir, 1, boxes), F32),
            pltpu.VMEM((dirs, terms, inside), jnp.int32),
            pltpu.VMEM((dirs, terms, inside), jnp.int32),
            pltpu.VMEM((2, list_width, boxes), jnp.int32),
            pltpu.VMEM((1, boxes), jnp.int32),
            pltpu.VMEM((2, list_width, LANES), jnp.int32),
            pltpu.VMEM(phases.shape, F32),
            pltpu.VMEM(fine_ops.shape, BF16),
            pltpu.VMEM(coarse_ops.shape, BF16),
            pltpu.VMEM((dirs // 2,) + coarse_ops.shape[1:], BF16),
            pltpu.VMEM((inside, dirs * terms), F32),
            pltpu.VMEM((2 * dirs, inside, group), BF16),
            pltpu.VMEM((members, group + 2 * boxes), BF16),
            pltpu.VMEM((2 * dirs, group, coeffs), F32),
            pltpu.VMEM((2 * dirs, group, coeffs), BF16),
            pltpu.VMEM((wedges, boxes, coeffs), BF16),
            pltpu.VMEM((2 * dirs * half, boxes, coeffs), BF16),
            pltpu.VMEM((dirs // 2, inside, coeffs), BF16),
            pltpu.VMEM((dirs // 2, inside, coeffs), BF16),
            pltpu.VMEM((boxes, coeffs), F32),
            pltpu.SemaphoreType.DMA((8,)),
        ] + [pltpu.SemaphoreType.DMA((n,)) for n in (1, 3, 1, 3, 1, 2, 4, 1)],
        compiler_params=pltpu.CompilerParams(
            collective_id=0, has_side_effects=True, vmem_limit_bytes=limit),
        name="translations",
    )(*[
        pltpu.with_memory_space_constraint(value, pltpu.HBM)
        for value in (
            multipoles, box_scale.reshape(1, boxes), lists, fine_list.T, wedge_index.T, list_count.reshape(1, boxes),
            phases, fine_ops, coarse_ops)
    ])
    return pl.pallas_call(
        settle,
        out_shape=tuple(jax.ShapeDtypeStruct(out.shape, out.dtype) for out in outs),
        in_specs=[pl.BlockSpec(memory_space=pltpu.VMEM)] * 2,
        out_specs=tuple(pl.BlockSpec(memory_space=pltpu.HBM) for _ in outs),
        scratch_shapes=[pltpu.SemaphoreType.DMA((2,))],
        name="settle",
    )(*[pltpu.with_memory_space_constraint(out, pltpu.VMEM) for out in outs])


def solution(mesh):
    return jax.shard_map(
        per_device,
        mesh=mesh,
        in_specs=(
            P(("space", "dir"), None),
            P(("space", "dir")),
            P(("space", "dir"), None),
            P(("space", "dir"), None),
            P(("space", "dir")),
            P(),
            P(),
            P("dir", "space", None),
            P("dir", None, None),
        ),
        out_specs=(P(("space", "dir"), None), P(None, ("space", "dir"), None)),
        check_vma=False,
    )
```
